768 devices in a mesh: proj: 3 (over z_hi), space: 256 (over y, x, z_lo, core).
Axes of the slice: x: 4, y: 8, z: 12 (z_hi: 3, z_lo: 4; z = z_hi * 4 + z_lo), core: 2. Of those that a mesh axis runs over, the one named last changes fastest.
Arguments:
- design: float32 [512, 64, 384], P('space', None, 'proj'), may hold values from 0.02 to 0.98
- solid_mask: int32 [512, 64, 384], P('space', None, 'proj'), may hold values 0 or 1
- void_mask: int32 [512, 64, 384], P('space', None, 'proj'), may hold values 0 or 1
- load_mask: int32 [512, 64, 384], P('space'), may hold values 0 or 1
- support_mask: int32 [512, 64, 384], P('space'), may hold values 0 or 1
- thresholds: int32 [3], P('proj'), may hold values from 300 to 700
- group_weight: float32 [3], P('proj'), may hold values from 0.5 to 2
Outputs:
- sensitivity: float32 [512, 64, 384], P('space', None, 'proj')
The draws below stay inside these ranges and needn't reach their ends.
All inputs are finite; a program needn't handle non-finite values. No bound on the sum of `solid_mask` or of `void_mask` or of `load_mask` or of `support_mask` on one device may be relied on, other than what follows from the above.
Results may differ from the reference program's by a relative error of at most 0.0001.
Values sent between devices are 32-bit elements; how exact they have to be, the bound alone decides.
A program may use at most 32 MiB of HBM per device.

```python
import math
import jax
import jax.numpy as jnp

NY = 64
NPROJ = 3
NX = 512
NZ = 384


def place_ends(values, rng, least, top_value):
    dims = values.shape
    index_at = [jax.random.randint(jax.random.fold_in(rng, axis), (), 0, dims[axis]) for axis in range(len(dims))]
    values = values.at[tuple(index_at)].set(least)
    longest = dims.index(max(dims))
    index_at[longest] = (index_at[longest] + 1) % dims[longest]
    return values.at[tuple(index_at)].set(top_value)


def shard_levels(own_key, shape, cuts, low, high):
    loudness = 1.0
    for dim, shards_of in cuts:
        heights = jax.random.uniform(jax.random.fold_in(jax.random.fold_in(own_key, 6), dim), (shards_of,), jnp.float32, low / len(cuts), high / len(cuts))
        loudness = loudness * jnp.repeat(jnp.exp(heights), shape[dim] // shards_of).reshape((-1,) + (1,) * (len(shape) - 1 - dim))
    return loudness


def setup_inputs(seed: int = 0) -> dict:
    seeds = jax.random.split(jax.random.key(seed), 8)
    design = jnp.clip(0.02 + 0.96000002 * jax.random.uniform(seeds[0], (NX, NY, NZ), jnp.float32) ** shard_levels(seeds[0], (NX, NY, NZ), ((0, 256), (2, 3)), -0.2, 0.2), 0.02, 0.98)
    solid_mask = place_ends((jax.random.randint(seeds[1], (NX, NY, NZ), 0, 16) < 1).astype(jnp.int32), jax.random.fold_in(seeds[1], 1), 0, 1)
    void_mask = place_ends((jax.random.randint(seeds[2], (NX, NY, NZ), 0, 16) < 1).astype(jnp.int32), jax.random.fold_in(seeds[2], 1), 0, 1)
    load_mask = place_ends((jax.random.randint(seeds[3], (NX, NY, NZ), 0, 8) < 1).astype(jnp.int32), jax.random.fold_in(seeds[3], 1), 0, 1)
    support_mask = place_ends((jax.random.randint(seeds[4], (NX, NY, NZ), 0, 16) < 1).astype(jnp.int32), jax.random.fold_in(seeds[4], 1), 0, 1)
    thresholds = jax.random.randint(seeds[5], (NPROJ,), 300, 701).astype(jnp.int32)
    group_weight = jnp.clip(jnp.exp(math.log(2.0) - 1.3862944 * jax.random.uniform(seeds[6], (NPROJ,), jnp.float32) ** shard_levels(seeds[6], (NPROJ,), ((0, 3),), -0.2, 0.2)), 0.5, 2.0)
    return {"design": design, "solid_mask": solid_mask, "void_mask": void_mask, "load_mask": load_mask, "support_mask": support_mask, "thresholds": thresholds, "group_weight": group_weight}


RMIN = 2.0
BETA = 8.0
EMIN = 0.05
PENALTY = 4.0

def conic(padded):
    rows_x, rows_y, rows_z = padded.shape
    total = jnp.zeros((rows_x - 2, rows_y - 2, rows_z - 2), padded.dtype)
    for step_x in range(3):
        for step_y in range(3):
            for step_z in range(3):
                spread = (step_x - 1) * (step_x - 1) + (step_y - 1) * (step_y - 1) + (step_z - 1) * (step_z - 1)
                weight = RMIN - math.sqrt(spread)
                total = total + weight * padded[step_x:step_x + rows_x - 2, step_y:step_y + rows_y - 2, step_z:step_z + rows_z - 2]
    return total

def project(filtered, eta):
    bottom = jnp.tanh(BETA * eta) + jnp.tanh(BETA * (1.0 - eta))
    inner = jnp.tanh(BETA * (filtered - eta))
    return ((jnp.tanh(BETA * eta) + inner) / bottom, BETA * (1.0 - inner * inner) / bottom)

def neighbours(field_x):
    centre = field_x[1:-1]
    padded = jnp.pad(centre, ((0, 0), (1, 1), (1, 1)))
    others = [field_x[2:], field_x[:-2], padded[:, 2:, 1:-1], padded[:, :-2, 1:-1], padded[:, 1:-1, 2:], padded[:, 1:-1, :-2]]
    return (centre, others)

def conductance(stiff_x):
    centre, others = neighbours(stiff_x)
    return [0.5 * (centre + other) for other in others]

def operate(links, field_x):
    centre, others = neighbours(field_x)
    total = jnp.zeros_like(centre)
    for link, other in zip(links, others):
        total = total + link * (centre - other)
    return total

def energy(field_x):
    centre, others = neighbours(field_x)
    total = jnp.zeros_like(centre)
    for other in others:
        total = total + (centre - other) * (centre - other)
    return -0.5 * total

def extend(field):
    return jnp.pad(field, ((1, 1), (0, 0), (0, 0)))

def reference(design, solid_mask, void_mask, load_mask, support_mask, thresholds, group_weight):
    fixed = jnp.where(solid_mask == 1, jnp.ones_like(design), jnp.where(void_mask == 1, jnp.zeros_like(design), design))
    filtered = conic(jnp.pad(fixed, 1)) / conic(jnp.pad(jnp.ones_like(design), 1))
    load = load_mask.astype(design.dtype)
    support = support_mask.astype(design.dtype)
    sensitivity = jnp.zeros_like(design)
    for group in range(NPROJ):
        eta = thresholds[group].astype(design.dtype) / 1000.0
        value, slope = project(filtered, eta)
        stiff = EMIN + (1.0 - EMIN) * value * value * value
        links = conductance(extend(stiff))
        diag = sum(links) + PENALTY * support
        resid = load
        precond = resid / diag
        rz_now = jnp.sum(resid * precond)
        first = extend(precond)
        image = operate(links, first)
        step_one = rz_now / jnp.sum(precond * image)
        solution = step_one * first
        resid = resid - step_one * image
        precond = resid / diag
        rz_next = jnp.sum(resid * precond)
        second = extend(precond) + rz_next / rz_now * first
        image = operate(links, second)
        step_two = rz_next / jnp.sum(second[1:-1] * image)
        solution = solution + step_two * second
        sensitivity = sensitivity + group_weight[group] * energy(solution) * (3.0 * (1.0 - EMIN)) * value * value * slope
    return sensitivity
```

```python
import math

import jax
import jax.numpy as jnp
from jax import lax
from jax.experimental import pallas as pl
from jax.experimental.pallas import tpu as pltpu
from jax.sharding import PartitionSpec as P

RMIN = 2.0
BETA = 8.0
EMIN = 0.05
PENALTY = 4.0
MESH = pl.DeviceIdType.MESH
F32 = jnp.float32

NPROJ, NSPACE = 3, 256
NYC, NXC, NZLO, NCORE = 8, 4, 4, 2
NZC = NPROJ * NZLO
DEPTH, WIDTH, THICK = 2, 64, 128
GX, GZ = NSPACE * DEPTH, NPROJ * THICK

LO, HI = 16, 16 + THICK
ROWS = HI + 16
EDGE = 2.0 - math.sqrt(2.0)
CORNER = 2.0 - math.sqrt(3.0)
OWN = [(LO + i, 32) for i in range(0, THICK, 32)]
ALL = [(LO - 8, 8)] + OWN + [(HI, 8)]


def kernel(
    design, solid, void, load_in, support_in, eta_in, weight_in, out,
    raw, masks, fb, ls, ring, lr, sr, inm, inv, tw, tanhs, hh, cond, zz, idg, ww, uu, kk, rowa, rowb, rowc, done,
    in_sem, send_f, recv_f, send_e, recv_e, send_m, recv_m, send_t, recv_t,
    send_a, recv_a, send_b, recv_b, send_c, recv_c,
):
    me = lax.axis_index("space")
    slab = lax.axis_index("proj")
    core = me % NCORE
    zlo = (me // NCORE) % NZLO
    xc = (me // (NCORE * NZLO)) % NXC
    line_a = xc * NCORE + core
    line_z = slab * NZLO + zlo

    def space_at(step):
        return (me + (NSPACE + step)) % NSPACE

    def slab_at(step):
        return (slab + (NPROJ + step)) % NPROJ

    def at_a(step):
        other = (line_a + step) % (NXC * NCORE)
        return (slab, me + ((other // NCORE - xc) * (NCORE * NZLO) + (other % NCORE - core)))

    def at_b(step):
        return (slab, (me + step * (NSPACE // NYC)) % NSPACE)

    def at_c(step):
        other = (line_z + step) % NZC
        return (other // NZLO, me + (other % NZLO - zlo) * NCORE)

    near = (1, -1, 2, -2)
    halo = [(slab, space_at(d)) for d in near]
    halo += [(slab_at(e), space_at(d)) for d in (0,) + near for e in (1, -1)]
    partners = halo + [at_a(d) for d in range(1, 8)] + [at_b(d) for d in range(1, 8)] + [at_c(d) for d in range(1, 12)]

    barrier = pltpu.get_barrier_semaphore()
    for place in partners:
        pl.semaphore_signal(barrier, inc=1, device_id=place, device_id_type=MESH)

    loads = []
    for i, source in enumerate((design, solid, void)):
        target = raw if i == 0 else masks.at[i - 1]
        loads.append(pltpu.make_async_copy(source, target, in_sem.at[i]))
    for i, source in enumerate((load_in, support_in)):
        for j, step in enumerate((-1, 0, 1)):
            lane = pl.multiple_of(slab_at(step) * THICK, THICK)
            loads.append(
                pltpu.make_async_copy(source.at[:, :, pl.ds(lane, THICK)], masks.at[2 + 3 * i + j], in_sem.at[3 + 3 * i + j])
            )
    for item in loads:
        item.start()

    lane = lax.broadcasted_iota(jnp.int32, (1, 128), 1)
    cell_y = lane % WIDTH
    upper = lane >= WIDTH
    has_up = cell_y < WIDTH - 1
    has_down = cell_y > 0

    def y_up(v):
        return jnp.where(has_up, pltpu.roll(v, 127, 1), 0.0)

    def y_down(v):
        return jnp.where(has_down, pltpu.roll(v, 1, 1), 0.0)

    def swap(v):
        return pltpu.roll(v, WIDTH, 1)

    count_y = has_up.astype(F32) + has_down.astype(F32)
    for k in range(5):
        layer = jnp.where(upper, 1 + k, -k) + me * DEPTH
        in_x = ((layer >= 0) & (layer < GX)).astype(F32)
        count_x = (layer > 0).astype(F32) + (layer < GX - 1).astype(F32)
        for r0, n in ALL:
            z = slab * THICK + (r0 - LO) + lax.broadcasted_iota(jnp.int32, (n, 128), 0)
            in_z = ((z >= 0) & (z < GZ)).astype(F32)
            inm[k, r0 : r0 + n, :] = in_z * in_x
            if k < 4:
                count_z = (z > 0).astype(F32) + (z < GZ - 1).astype(F32)
                pair = count_y * count_z
                total = 2.0 + count_x + count_y + count_z
                total = total + EDGE * (count_x * (count_y + count_z) + pair) + CORNER * (count_x * pair)
                inv[k, r0 : r0 + n, :] = BETA / total

    eta = eta_in[0].astype(F32) / 1000.0
    row = lax.broadcasted_iota(jnp.int32, (8, 128), 0)
    tw[slab] = jnp.where(row == 0, eta, weight_in[0])

    for item in loads[:3]:
        item.wait()
    fixed = jnp.where(masks[0] == 1, 1.0, jnp.where(masks[1] == 1, 0.0, raw[...]))
    fb[2, LO:HI, :] = fixed.reshape(128, 128).T
    for item in loads[3:]:
        item.wait()
    for i in range(2):
        for j in range(3):
            turned = masks[2 + 3 * i + j].reshape(128, 128).astype(F32).T
            if j == 0:
                ls[1, i, LO - 8 : LO, :] = turned[120:, :]
            elif j == 1:
                ls[1, i, LO:HI, :] = turned
            else:
                ls[1, i, HI : HI + 8, :] = turned[:8, :]

    pl.semaphore_wait(barrier, len(partners))

    def remote(source, target, ssem, rsem, place):
        return pltpu.make_async_remote_copy(
            src_ref=source, dst_ref=target, send_sem=ssem, recv_sem=rsem, device_id=place, device_id_type=MESH
        )

    main, rims, marks, small = [], [], [], []
    for i, d in enumerate(near):
        main.append(
            remote(fb.at[2, pl.ds(LO, THICK), :], fb.at[2 - d, pl.ds(LO, THICK), :], send_f.at[i], recv_f.at[i], (slab, space_at(d)))
        )
    for i, d in enumerate((0,) + near):
        for j, e in enumerate((1, -1)):
            src, dst = (HI - 8, LO - 8) if e == 1 else (LO, HI)
            rims.append(
                remote(
                    fb.at[2, pl.ds(src, 8), :], fb.at[2 - d, pl.ds(dst, 8), :],
                    send_e.at[2 * i + j], recv_e.at[2 * i + j], (slab_at(e), space_at(d)),
                )
            )
    for i, d in enumerate((1, -1)):
        marks.append(
            remote(
                ls.at[1, :, pl.ds(LO - 8, THICK + 16), :], ls.at[1 - d, :, pl.ds(LO - 8, THICK + 16), :],
                send_m.at[i], recv_m.at[i], (slab, space_at(d)),
            )
        )
    for i, e in enumerate((1, -1)):
        small.append(remote(tw.at[slab], tw.at[slab], send_t.at[i], recv_t.at[i], (slab_at(e), me)))
    copies = main[:2] + small + rims + main[2:] + marks
    for item in copies:
        item.start()
    for item in main + small + rims:
        item.wait_recv()

    for r0, n in ALL:
        rows = slice(r0, r0 + n)
        ring[0, rows, :] = fb[2, rows, :] * inm[0, rows, :]
        p1, m1, p2, m2 = fb[3, rows, :], fb[1, rows, :], fb[4, rows, :], fb[0, rows, :]
        ring[1, rows, :] = swap(jnp.where(upper, m1, p1)) * inm[1, rows, :]
        ring[2, rows, :] = jnp.where(upper, p1, m1) * inm[2, rows, :]
        ring[3, rows, :] = swap(jnp.where(upper, m2, p2)) * inm[3, rows, :]
        ring[4, rows, :] = jnp.where(upper, p2, m2) * inm[4, rows, :]

    etas, tops, scales, weights = [], [], [], []
    for g in range(NPROJ):
        e = tw[g, 0:1, :]
        t = jnp.tanh(BETA * e)
        bottom = t + jnp.tanh(BETA * (1.0 - e))
        etas.append(BETA * e)
        tops.append(t / bottom)
        scales.append(1.0 / bottom)
        weights.append(tw[g, 1:2, :] * (-0.5 * 3.0 * (1.0 - EMIN) * BETA) / bottom)

    for r0, n in ALL:
        rows = slice(r0, r0 + n)
        centre, side = [], []
        for k in range(5):
            v = ring[k, rows, :]
            zb = ring[k, r0 + 1 : r0 + n + 1, :] + ring[k, r0 - 1 : r0 + n - 1, :]
            yb = y_up(v) + y_down(v)
            cross = y_up(zb) + y_down(zb)
            faces = zb + yb
            if k < 4:
                centre.append(2.0 * v + faces + EDGE * cross)
            side.append(v + EDGE * faces + CORNER * cross)
        for k in range(4):
            inner = side[k - 1] if k else swap(side[0])
            f8 = (centre[k] + (inner + side[k + 1])) * inv[k, rows, :]
            mask = inm[k, rows, :]
            for g in range(NPROJ):
                t = jnp.tanh(f8 - etas[g])
                value = t * scales[g] + tops[g]
                square = value * value
                hh[g, k, rows, :] = ((0.5 * (1.0 - EMIN)) * (square * value) + 0.5 * EMIN) * mask
                if k == 0 and LO <= r0 < HI:
                    kk[g, r0 - LO : r0 - LO + n, :] = (weights[g] * square) * (1.0 - t * t)

    for item in marks:
        item.wait_recv()

    for r0, n in ALL:
        rows = slice(r0, r0 + n)
        for k in range(3):
            mask = inm[k, rows, :]
            both = []
            for i in range(2):
                if k == 0:
                    both.append(ls[1, i, rows, :])
                elif k == 1:
                    both.append(swap(jnp.where(upper, ls[0, i, rows, :], ls[2, i, rows, :])))
                else:
                    both.append(jnp.where(upper, ls[2, i, rows, :], ls[0, i, rows, :]))
            lr[k, rows, :] = both[0] * mask
            sr[k, rows, :] = PENALTY * jnp.maximum(both[1], 1.0 - mask)

    for g in range(NPROJ):
        for k in range(3):
            for r0, n in ALL:
                rows = slice(r0, r0 + n)
                h = hh[g, k, rows, :]
                inner = hh[g, k - 1, rows, :] if k else swap(h)
                links = [
                    h + inner,
                    h + hh[g, k + 1, rows, :],
                    h + y_up(h),
                    h + y_down(h),
                    h + hh[g, k, r0 + 1 : r0 + n + 1, :],
                    h + hh[g, k, r0 - 1 : r0 + n - 1, :],
                ]
                diag = sr[k, rows, :]
                for i, link in enumerate(links):
                    diag = diag + link
                    if k < 2:
                        cond[g, k, i, rows, :] = link
                inverse = inm[k, rows, :] / diag
                zz[g, k, rows, :] = lr[k, rows, :] * inverse
                if k < 2:
                    idg[g, k, rows, :] = inverse

    def others(field, g, k, r0, n, v):
        rows = slice(r0, r0 + n)
        return [
            field[g, k - 1, rows, :] if k else swap(v),
            field[g, k + 1, rows, :],
            y_up(v),
            y_down(v),
            field[g, k, r0 + 1 : r0 + n + 1, :],
            field[g, k, r0 - 1 : r0 + n - 1, :],
        ]

    def operate(field, g, k, r0, n):
        v = field[g, k, r0 : r0 + n, :]
        total = None
        for i, other in enumerate(others(field, g, k, r0, n, v)):
            term = cond[g, k, i, r0 : r0 + n, :] * (v - other)
            total = term if total is None else total + term
        return v, total

    def fold(v):
        return jnp.sum(v.reshape(v.shape[0] // 8, 8, 128), axis=0)

    sums = [[jnp.zeros((8, 128), F32) for _ in range(4)] for _ in range(NPROJ)]
    for g in range(NPROJ):
        for k in range(2):
            for r0, n in ALL:
                rows = slice(r0, r0 + n)
                v, image = operate(zz, g, k, r0, n)
                w = image * idg[g, k, rows, :]
                ww[g, k, rows, :] = w
                if k == 0 and LO <= r0 < HI:
                    sums[g][0] = sums[g][0] + fold(v * lr[0, rows, :])
                    sums[g][1] = sums[g][1] + fold(v * image)
                    sums[g][2] = sums[g][2] + fold(w * image)
        for r0, n in OWN:
            w, image = operate(ww, g, 0, r0, n)
            sums[g][3] = sums[g][3] + fold(w * image)

    parts = jnp.concatenate([jnp.sum(sums[g][i], axis=0, keepdims=True) for i in range(4) for g in range(NPROJ)] + [jnp.zeros((4, 128), F32)], axis=0)
    totals = jnp.sum(parts, axis=1, keepdims=True)
    which = lax.broadcasted_iota(jnp.int32, (16, 128), 0)
    place = (which // NPROJ) * 32 + which % NPROJ
    spot = lax.broadcasted_iota(jnp.int32, (16, 128), 1)
    line = jnp.sum(jnp.where((spot == place) & (which < 12), totals, 0.0), axis=0, keepdims=True)

    def share(value, rows_ref, ssem, rsem, target, size):
        rows_ref[0] = value
        items = [remote(rows_ref.at[0], rows_ref.at[d], ssem.at[d], rsem.at[d], target(d)) for d in range(1, size)]
        for item in items:
            item.start()
        for item in items:
            item.wait_recv()
        total = rows_ref[0]
        for d in range(1, size):
            total = total + rows_ref[d]
        return total, items

    line, items_a = share(line, rowa, send_a, recv_a, at_a, NXC * NCORE)
    line, items_b = share(line, rowb, send_b, recv_b, at_b, NYC)
    line, items_c = share(line, rowc, send_c, recv_c, at_c, NZC)

    rz0, pq1 = line, pltpu.roll(line, 96, 1)
    qdq, wsw = pltpu.roll(line, 64, 1), pltpu.roll(line, 32, 1)
    step_one = rz0 / pq1
    rz1 = rz0 - 2.0 * step_one * pq1 + step_one * step_one * qdq
    grow = 1.0 + rz1 / rz0
    pq2 = grow * grow * pq1 - 2.0 * grow * step_one * qdq + step_one * step_one * wsw
    step_two = rz1 / pq2
    along = step_one + step_two * grow
    across = -step_one * step_two

    for g in range(NPROJ):
        one = jnp.broadcast_to(along[:, g : g + 1], (1, 128))
        two = jnp.broadcast_to(across[:, g : g + 1], (1, 128))
        for k in range(2):
            for r0, n in ALL if k == 0 else OWN:
                rows = slice(r0, r0 + n)
                uu[g, k, rows, :] = one * zz[g, k, rows, :] + two * ww[g, k, rows, :]
    for r0, n in OWN:
        result = None
        for g in range(NPROJ):
            v = uu[g, 0, r0 : r0 + n, :]
            total = None
            for other in others(uu, g, 0, r0, n, v):
                gap = v - other
                total = gap * gap if total is None else total + gap * gap
            term = kk[g, r0 - LO : r0 - LO + n, :] * total
            result = term if result is None else result + term
        done[r0 - LO : r0 - LO + n, :] = result
    out[...] = done[...].T.reshape(DEPTH, WIDTH, THICK)

    for item in copies + items_a + items_b + items_c:
        item.wait_send()


def local(design, solid_mask, void_mask, load_mask, support_mask, thresholds, group_weight):
    dma = pltpu.SemaphoreType.DMA
    return pl.pallas_call(
        kernel,
        out_shape=jax.ShapeDtypeStruct((DEPTH, WIDTH, THICK), F32),
        in_specs=[pl.BlockSpec(memory_space=pl.ANY)] * 5 + [pl.BlockSpec(memory_space=pltpu.SMEM)] * 2,
        out_specs=pl.BlockSpec(memory_space=pltpu.VMEM),
        scratch_shapes=[
            pltpu.VMEM((DEPTH, WIDTH, THICK), F32),
            pltpu.VMEM((8, DEPTH, WIDTH, THICK), jnp.int32),
            pltpu.VMEM((5, ROWS, 128), F32),
            pltpu.VMEM((3, 2, ROWS, 128), F32),
            pltpu.VMEM((5, ROWS, 128), F32),
            pltpu.VMEM((3, ROWS, 128), F32),
            pltpu.VMEM((3, ROWS, 128), F32),
            pltpu.VMEM((5, ROWS, 128), F32),
            pltpu.VMEM((4, ROWS, 128), F32),
            pltpu.VMEM((NPROJ, 8, 128), F32),
            pltpu.VMEM((8, 128), F32),
            pltpu.VMEM((NPROJ, 4, ROWS, 128), F32),
            pltpu.VMEM((NPROJ, 2, 6, ROWS, 128), F32),
            pltpu.VMEM((NPROJ, 3, ROWS, 128), F32),
            pltpu.VMEM((NPROJ, 2, ROWS, 128), F32),
            pltpu.VMEM((NPROJ, 2, ROWS, 128), F32),
            pltpu.VMEM((NPROJ, 2, ROWS, 128), F32),
            pltpu.VMEM((NPROJ, THICK, 128), F32),
            pltpu.VMEM((8, 1, 128), F32),
            pltpu.VMEM((8, 1, 128), F32),
            pltpu.VMEM((12, 1, 128), F32),
            pltpu.VMEM((THICK, 128), F32),
            dma((9,)),
            dma((4,)), dma((4,)),
            dma((10,)), dma((10,)),
            dma((2,)), dma((2,)),
            dma((2,)), dma((2,)),
            dma((8,)), dma((8,)),
            dma((8,)), dma((8,)),
            dma((12,)), dma((12,)),
        ],
        compiler_params=pltpu.CompilerParams(collective_id=0, has_side_effects=True),
    )(design, solid_mask, void_mask, load_mask, support_mask, thresholds, group_weight)


def solution(mesh):
    placed = (
        P("space", None, "proj"),
        P("space", None, "proj"),
        P("space", None, "proj"),
        P("space", None, None),
        P("space", None, None),
        P("proj"),
        P("proj"),
    )
    return jax.shard_map(
        local, mesh=mesh, in_specs=placed, out_specs=P("space", None, "proj"), check_vma=False
    )
```

```python
import math

import jax
import jax.numpy as jnp
from jax import lax
from jax.experimental import pallas as pl
from jax.experimental.pallas import tpu as pltpu
from jax.sharding import PartitionSpec as P

RMIN = 2.0
BETA = 8.0
EMIN = 0.05
PENALTY = 4.0
MESH = pl.DeviceIdType.MESH
F32 = jnp.float32

NPROJ, NSPACE = 3, 256
NYC, NXC, NZLO, NCORE = 8, 4, 4, 2
NZC = NPROJ * NZLO
DEPTH, WIDTH, THICK = 2, 64, 128
GX, GZ = NSPACE * DEPTH, NPROJ * THICK

LO, HI = 16, 16 + THICK
ROWS = HI + 16
EDGE = 2.0 - math.sqrt(2.0)
CORNER = 2.0 - math.sqrt(3.0)
OWN = [(LO + i, 32) for i in range(0, THICK, 32)]
ALL = [(LO - 8, 8)] + OWN + [(HI, 8)]


def kernel(
    design, solid, void, load_in, support_in, eta_in, weight_in, out,
    raw, masks, fb, lt, ls, ring, lr, sr, inm, inv, tw, hh, cond, zz, idg, ww, uu, kk, rowp, rowz, done,
    in_sem, send_f, recv_f, send_e, recv_e, send_m, recv_m, send_t, recv_t,
    send_p, recv_p, send_z, recv_z,
):
    me = lax.axis_index("space")
    slab = lax.axis_index("proj")
    core = me & 1
    zlo = (me >> 1) & 3
    line_z = slab * NZLO + zlo
    inward = 1 - 2 * core
    slab_up = jnp.where(slab == NPROJ - 1, 0, slab + 1)
    slab_down = jnp.where(slab == 0, NPROJ - 1, slab - 1)
    slabs = {0: slab, 1: slab_up, -1: slab_down}

    def space_at(step):
        return (me + step) & (NSPACE - 1)

    loads = []
    for i, source in enumerate((design, solid, void)):
        target = raw if i == 0 else masks.at[i - 1]
        loads.append(pltpu.make_async_copy(source, target, in_sem.at[i]))
    for i, source in enumerate((load_in, support_in)):
        for j, step in enumerate((-1, 0, 1)):
            lane = pl.multiple_of(slabs[step] * THICK, THICK)
            loads.append(
                pltpu.make_async_copy(source.at[:, :, pl.ds(lane, THICK)], masks.at[2 + 3 * i + j], in_sem.at[3 + 3 * i + j])
            )
    for item in loads[:3]:
        item.start()

    near = (1, -1, 2, -2)
    halo = [(slabs[e], space_at(d)) for d in near[::-1] + (0,) for e in (1, -1)]
    halo += [(slab, space_at(d)) for d in near]
    rows_y = [(me + (dy << 5)) & 0xE0 for dy in range(NYC)]
    rows_x = [(me + (dx << 3)) & 0x18 for dx in range(NXC)]
    low = me & 0x07
    plane = sorted(
        ((dy, dx) for dy in range(NYC) for dx in range(NXC) if dy or dx),
        key=lambda p: -(min(p[0], NYC - p[0]) + min(p[1], NXC - p[1])),
    )
    plane = [(slab, rows_y[dy] + rows_x[dx] + low) for dy, dx in plane]
    stack = sorted(((dz, dc) for dz in range(NZC) for dc in range(NCORE) if dz or dc), key=lambda p: -min(p[0], NZC - p[0]))
    base = me & 0xF8
    cores = (core, 1 - core)
    levels = []
    for dz in range(NZC):
        z = line_z + dz
        z = jnp.where(z >= NZC, z - NZC, z)
        levels.append((z >> 2, base + ((z & 3) << 1)))
    stack = [(levels[dz][0], levels[dz][1] + cores[dc]) for dz, dc in stack]
    partners = halo + plane + stack

    barrier = pltpu.get_barrier_semaphore()
    for place in partners:
        pl.semaphore_signal(barrier, inc=1, device_id=place, device_id_type=MESH)
    for item in loads[3:]:
        item.start()

    lane = lax.broadcasted_iota(jnp.int32, (1, 128), 1)
    cell_y = lane % WIDTH
    upper = lane >= WIDTH
    has_up = cell_y < WIDTH - 1
    has_down = cell_y > 0

    def y_up(v):
        return jnp.where(has_up, pltpu.roll(v, 127, 1), 0.0)

    def y_down(v):
        return jnp.where(has_down, pltpu.roll(v, 1, 1), 0.0)

    def swap(v):
        return pltpu.roll(v, WIDTH, 1)

    eta = eta_in[0].astype(F32) / 1000.0
    row = lax.broadcasted_iota(jnp.int32, (8, 128), 0)
    tw[slab] = jnp.where(row == 0, eta, weight_in[0])

    for item in loads[:3]:
        item.wait()
    fixed = jnp.where(masks[0] == 1, 1.0, jnp.where(masks[1] == 1, 0.0, raw[...]))
    fb[2, LO:HI, :] = fixed.reshape(128, 128).T

    def remote(source, target, ssem, rsem, place):
        return pltpu.make_async_remote_copy(
            src_ref=source, dst_ref=target, send_sem=ssem, recv_sem=rsem, device_id=place, device_id_type=MESH
        )

    def main_copy(i, source, target, step):
        return remote(
            fb.at[source, pl.ds(LO, THICK), :], fb.at[target, pl.ds(LO, THICK), :],
            send_f.at[i], recv_f.at[i], (slab, space_at(step)),
        )

    from_outer = main_copy(0, 2, 2 + inward, -inward)
    from_far = main_copy(1, 2, 2 - 2 * inward, 2 * inward)
    from_partner = main_copy(2, 2, 2 - inward, inward)
    relay = main_copy(3, 2 - inward, 2 - 2 * inward, inward)
    rims, marks, small = [], [], []
    for i, d in enumerate(near[::-1] + (0,)):
        for j, e in enumerate((1, -1)):
            src, dst = (HI - 8, LO - 8) if e == 1 else (LO, HI)
            rims.append(
                remote(
                    fb.at[2, pl.ds(src, 8), :], fb.at[2 - d, pl.ds(dst, 8), :],
                    send_e.at[2 * i + j], recv_e.at[2 * i + j], (slabs[e], space_at(d)),
                )
            )
    for i, e in enumerate((1, -1)):
        small.append(remote(tw.at[slab], tw.at[slab], send_t.at[i], recv_t.at[i], (slabs[e], me)))

    spill_up = ((me & 7) == 7).astype(jnp.int32)
    spill_down = ((me & 7) == 0).astype(jnp.int32)
    for i, (d, spill) in enumerate(((1, spill_up), (-1, -spill_down))):
        start = pl.multiple_of(THICK + THICK * spill, 8)
        place = jnp.where(spill == 0, slab, slabs[d])
        marks.append(
            remote(
                lt.at[:, pl.ds(start, THICK + 16), :], ls.at[i, :, pl.ds(LO - 8, THICK + 16), :],
                send_m.at[i], recv_m.at[i], (place, space_at(d)),
            )
        )

    pl.semaphore_wait(barrier, len(partners))
    for item in rims[:8] + [from_outer, from_far, from_partner] + rims[8:] + small:
        item.start()

    for item in loads[3:]:
        item.wait()
    for i in range(2):
        for j in range(3):
            turned = masks[2 + 3 * i + j].reshape(128, 128).astype(F32).T
            lt[i, 8 + THICK * j : 8 + THICK * (j + 1), :] = turned
            if j == 0:
                lt[i, 8 + 3 * THICK :, :] = turned[:8, :]
            if j == 2:
                lt[i, 0:8, :] = turned[120:, :]
    for item in marks:
        item.start()

    count_y = has_up.astype(F32) + has_down.astype(F32)
    for k in range(5):
        layer = jnp.where(upper, 1 + k, -k) + me * DEPTH
        in_x = ((layer >= 0) & (layer < GX)).astype(F32)
        count_x = (layer > 0).astype(F32) + (layer < GX - 1).astype(F32)
        for r0, n in ALL:
            z = slab * THICK + (r0 - LO) + lax.broadcasted_iota(jnp.int32, (n, 128), 0)
            in_z = ((z >= 0) & (z < GZ)).astype(F32)
            inm[k, r0 : r0 + n, :] = in_z * in_x
            if k < 4:
                count_z = (z > 0).astype(F32) + (z < GZ - 1).astype(F32)
                pair = count_y * count_z
                total = 2.0 + count_x + count_y + count_z
                total = total + EDGE * (count_x * (count_y + count_z) + pair) + CORNER * (count_x * pair)
                inv[k, r0 : r0 + n, :] = BETA / total

    from_outer.wait_recv()
    relay.start()
    for item in [from_far, from_partner] + small + rims:
        item.wait_recv()
    relay.wait_recv()

    for r0, n in ALL:
        rows = slice(r0, r0 + n)
        ring[0, rows, :] = fb[2, rows, :] * inm[0, rows, :]
        p1, m1, p2, m2 = fb[3, rows, :], fb[1, rows, :], fb[4, rows, :], fb[0, rows, :]
        ring[1, rows, :] = swap(jnp.where(upper, m1, p1)) * inm[1, rows, :]
        ring[2, rows, :] = jnp.where(upper, p1, m1) * inm[2, rows, :]
        ring[3, rows, :] = swap(jnp.where(upper, m2, p2)) * inm[3, rows, :]
        ring[4, rows, :] = jnp.where(upper, p2, m2) * inm[4, rows, :]

    etas, tops, scales, weights = [], [], [], []
    for g in range(NPROJ):
        e = tw[g, 0:1, :]
        t = jnp.tanh(BETA * e)
        bottom = t + jnp.tanh(BETA * (1.0 - e))
        etas.append(BETA * e)
        tops.append(t / bottom)
        scales.append(1.0 / bottom)
        weights.append(tw[g, 1:2, :] * (-0.5 * 3.0 * (1.0 - EMIN) * BETA) / bottom)

    for r0, n in ALL:
        rows = slice(r0, r0 + n)
        centre, side = [], []
        for k in range(5):
            v = ring[k, rows, :]
            zb = ring[k, r0 + 1 : r0 + n + 1, :] + ring[k, r0 - 1 : r0 + n - 1, :]
            yb = y_up(v) + y_down(v)
            cross = y_up(zb) + y_down(zb)
            faces = zb + yb
            if k < 4:
                centre.append(2.0 * v + faces + EDGE * cross)
            side.append(v + EDGE * faces + CORNER * cross)
        for k in range(4):
            inner = side[k - 1] if k else swap(side[0])
            f8 = (centre[k] + (inner + side[k + 1])) * inv[k, rows, :]
            mask = inm[k, rows, :]
            for g in range(NPROJ):
                t = jnp.tanh(f8 - etas[g])
                value = t * scales[g] + tops[g]
                square = value * value
                hh[g, k, rows, :] = ((0.5 * (1.0 - EMIN)) * (square * value) + 0.5 * EMIN) * mask
                if k == 0 and LO <= r0 < HI:
                    kk[g, r0 - LO : r0 - LO + n, :] = (weights[g] * square) * (1.0 - t * t)

    for item in marks:
        item.wait_recv()

    for r0, n in ALL:
        rows = slice(r0, r0 + n)
        for k in range(3):
            mask = inm[k, rows, :]
            both = []
            for i in range(2):
                if k == 0:
                    both.append(lt[i, r0 + 8 + THICK - LO : r0 + n + 8 + THICK - LO, :])
                elif k == 1:
                    both.append(swap(jnp.where(upper, ls[0, i, rows, :], ls[1, i, rows, :])))
                else:
                    both.append(jnp.where(upper, ls[1, i, rows, :], ls[0, i, rows, :]))
            lr[k, rows, :] = both[0] * mask
            sr[k, rows, :] = PENALTY * jnp.maximum(both[1], 1.0 - mask)

    for g in range(NPROJ):
        for k in range(3):
            for r0, n in ALL:
                rows = slice(r0, r0 + n)
                h = hh[g, k, rows, :]
                inner = hh[g, k - 1, rows, :] if k else swap(h)
                links = [
                    h + inner,
                    h + hh[g, k + 1, rows, :],
                    h + y_up(h),
                    h + y_down(h),
                    h + hh[g, k, r0 + 1 : r0 + n + 1, :],
                    h + hh[g, k, r0 - 1 : r0 + n - 1, :],
                ]
                diag = sr[k, rows, :]
                for i, link in enumerate(links):
                    diag = diag + link
                    if k < 2:
                        cond[g, k, i, rows, :] = link
                inverse = inm[k, rows, :] / diag
                zz[g, k, rows, :] = lr[k, rows, :] * inverse
                if k < 2:
                    idg[g, k, rows, :] = inverse

    def others(field, g, k, r0, n, v):
        rows = slice(r0, r0 + n)
        return [
            field[g, k - 1, rows, :] if k else swap(v),
            field[g, k + 1, rows, :],
            y_up(v),
            y_down(v),
            field[g, k, r0 + 1 : r0 + n + 1, :],
            field[g, k, r0 - 1 : r0 + n - 1, :],
        ]

    def operate(field, g, k, r0, n):
        v = field[g, k, r0 : r0 + n, :]
        total = None
        for i, other in enumerate(others(field, g, k, r0, n, v)):
            term = cond[g, k, i, r0 : r0 + n, :] * (v - other)
            total = term if total is None else total + term
        return v, total

    def fold(v):
        return jnp.sum(v.reshape(v.shape[0] // 8, 8, 128), axis=0)

    sums = [[jnp.zeros((8, 128), F32) for _ in range(4)] for _ in range(NPROJ)]
    for g in range(NPROJ):
        for k in range(2):
            for r0, n in ALL:
                rows = slice(r0, r0 + n)
                v, image = operate(zz, g, k, r0, n)
                w = image * idg[g, k, rows, :]
                ww[g, k, rows, :] = w
                if k == 0 and LO <= r0 < HI:
                    sums[g][0] = sums[g][0] + fold(v * lr[0, rows, :])
                    sums[g][1] = sums[g][1] + fold(v * image)
                    sums[g][2] = sums[g][2] + fold(w * image)
        for r0, n in OWN:
            w, image = operate(ww, g, 0, r0, n)
            sums[g][3] = sums[g][3] + fold(w * image)

    parts = jnp.concatenate([jnp.sum(sums[g][i], axis=0, keepdims=True) for i in range(4) for g in range(NPROJ)] + [jnp.zeros((4, 128), F32)], axis=0)
    totals = jnp.sum(parts, axis=1, keepdims=True)
    which = lax.broadcasted_iota(jnp.int32, (16, 128), 0)
    place = (which // NPROJ) * 32 + which % NPROJ
    spot = lax.broadcasted_iota(jnp.int32, (16, 128), 1)
    line = jnp.sum(jnp.where((spot == place) & (which < 12), totals, 0.0), axis=0, keepdims=True)

    def share(value, rows_ref, ssem, rsem, places):
        rows_ref[0] = value
        for d, place in enumerate(places):
            remote(rows_ref.at[0], rows_ref.at[d + 1], ssem.at[0], rsem.at[0], place).start()
        every = rows_ref.at[pl.ds(1, len(places))]
        return remote(every, every, ssem.at[0], rsem.at[0], places[0])

    def gathered(rows_ref, size):
        terms = [rows_ref[d] for d in range(size)]
        while len(terms) > 1:
            terms = [a + b for a, b in zip(terms[::2], terms[1::2])] + terms[len(terms) // 2 * 2 :]
        return terms[0]

    in_plane = share(line, rowp, send_p, recv_p, plane)
    for item in [from_outer, from_far, from_partner, relay] + rims + small + marks:
        item.wait_send()
    in_plane.wait_recv()
    in_stack = share(gathered(rowp, NXC * NYC), rowz, send_z, recv_z, stack)
    in_plane.wait_send()
    in_stack.wait_recv()
    line = gathered(rowz, NZC * NCORE)

    rz0, pq1 = line, pltpu.roll(line, 96, 1)
    qdq, wsw = pltpu.roll(line, 64, 1), pltpu.roll(line, 32, 1)
    step_one = rz0 / pq1
    rz1 = rz0 - 2.0 * step_one * pq1 + step_one * step_one * qdq
    grow = 1.0 + rz1 / rz0
    pq2 = grow * grow * pq1 - 2.0 * grow * step_one * qdq + step_one * step_one * wsw
    step_two = rz1 / pq2
    along = step_one + step_two * grow
    across = -step_one * step_two

    for g in range(NPROJ):
        one = jnp.broadcast_to(along[:, g : g + 1], (1, 128))
        two = jnp.broadcast_to(across[:, g : g + 1], (1, 128))
        for k in range(2):
            for r0, n in ALL if k == 0 else OWN:
                rows = slice(r0, r0 + n)
                uu[g, k, rows, :] = one * zz[g, k, rows, :] + two * ww[g, k, rows, :]
    for r0, n in OWN:
        result = None
        for g in range(NPROJ):
            v = uu[g, 0, r0 : r0 + n, :]
            total = None
            for other in others(uu, g, 0, r0, n, v):
                gap = v - other
                total = gap * gap if total is None else total + gap * gap
            term = kk[g, r0 - LO : r0 - LO + n, :] * total
            result = term if result is None else result + term
        done[r0 - LO : r0 - LO + n, :] = result
    out[...] = done[...].T.reshape(DEPTH, WIDTH, THICK)

    in_stack.wait_send()


def local(design, solid_mask, void_mask, load_mask, support_mask, thresholds, group_weight):
    dma = pltpu.SemaphoreType.DMA
    return pl.pallas_call(
        kernel,
        out_shape=jax.ShapeDtypeStruct((DEPTH, WIDTH, THICK), F32),
        in_specs=[pl.BlockSpec(memory_space=pl.ANY)] * 5 + [pl.BlockSpec(memory_space=pltpu.SMEM)] * 2,
        out_specs=pl.BlockSpec(memory_space=pltpu.VMEM),
        scratch_shapes=[
            pltpu.VMEM((DEPTH, WIDTH, THICK), F32),
            pltpu.VMEM((8, DEPTH, WIDTH, THICK), jnp.int32),
            pltpu.VMEM((5, ROWS, 128), F32),
            pltpu.VMEM((2, 3 * THICK + 16, 128), F32),
            pltpu.VMEM((2, 2, ROWS, 128), F32),
            pltpu.VMEM((5, ROWS, 128), F32),
            pltpu.VMEM((3, ROWS, 128), F32),
            pltpu.VMEM((3, ROWS, 128), F32),
            pltpu.VMEM((5, ROWS, 128), F32),
            pltpu.VMEM((4, ROWS, 128), F32),
            pltpu.VMEM((NPROJ, 8, 128), F32),
            pltpu.VMEM((NPROJ, 4, ROWS, 128), F32),
            pltpu.VMEM((NPROJ, 2, 6, ROWS, 128), F32),
            pltpu.VMEM((NPROJ, 3, ROWS, 128), F32),
            pltpu.VMEM((NPROJ, 2, ROWS, 128), F32),
            pltpu.VMEM((NPROJ, 2, ROWS, 128), F32),
            pltpu.VMEM((NPROJ, 2, ROWS, 128), F32),
            pltpu.VMEM((NPROJ, THICK, 128), F32),
            pltpu.VMEM((NXC * NYC, 1, 128), F32),
            pltpu.VMEM((NZC * NCORE, 1, 128), F32),
            pltpu.VMEM((THICK, 128), F32),
            dma((9,)),
            dma((4,)), dma((4,)),
            dma((10,)), dma((10,)),
            dma((2,)), dma((2,)),
            dma((2,)), dma((2,)),
            dma((1,)), dma((1,)),
            dma((1,)), dma((1,)),
        ],
        compiler_params=pltpu.CompilerParams(collective_id=0, has_side_effects=True),
    )(design, solid_mask, void_mask, load_mask, support_mask, thresholds, group_weight)


def solution(mesh):
    placed = (
        P("space", None, "proj"),
        P("space", None, "proj"),
        P("space", None, "proj"),
        P("space", None, None),
        P("space", None, None),
        P("proj"),
        P("proj"),
    )
    return jax.shard_map(
        local, mesh=mesh, in_specs=placed, out_specs=P("space", None, "proj"), check_vma=False
    )
```

```python
import math

import jax
import jax.numpy as jnp
from jax import lax
from jax.experimental import pallas as pl
from jax.experimental.pallas import tpu as pltpu
from jax.sharding import PartitionSpec as P

RMIN = 2.0
BETA = 8.0
EMIN = 0.05
PENALTY = 4.0
MESH = pl.DeviceIdType.MESH
F32 = jnp.float32

NPROJ, NSPACE = 3, 256
NYC, NXC, NZLO, NCORE = 8, 4, 4, 2
NZC = NPROJ * NZLO
DEPTH, WIDTH, THICK = 2, 64, 128
GX, GZ = NSPACE * DEPTH, NPROJ * THICK

LO, HI = 16, 16 + THICK
ROWS = HI + 16
EDGE = 2.0 - math.sqrt(2.0)
CORNER = 2.0 - math.sqrt(3.0)
OWN = [(LO + i, 32) for i in range(0, THICK, 32)]
RIM = [(LO - 8, 8), (HI, 8)]
ALL = RIM[:1] + OWN + RIM[1:]
FILTER = [(24, 40), (64, 40), (104, 32)], [(8, 16), (136, 16)]
DIAGONAL = [(32, 32), (64, 32), (96, 32)], [(8, 24), (128, 24)]
FIRST = [(40, 40), (80, 40)], [(8, 32), (120, 32)]
SECOND = [(48, 32), (80, 32)], [(16, 32), (112, 32)]


def kernel(
    design, solid, void, load_in, support_in, eta_in, weight_in, out,
    raw, masks, fb, lt, ls, ring, lr, sr, inm, inv, tw, hh, cond, zz, idg, ww, kk, rowp, rowz, ee, turned_e,
    in_sem, send_f, recv_f, send_e, recv_e, send_m, recv_m, send_t, recv_t,
    send_p, recv_p, send_z, recv_z,
):
    me = lax.axis_index("space")
    slab = lax.axis_index("proj")
    core = me & 1
    zlo = (me >> 1) & 3
    line_z = slab * NZLO + zlo
    inward = 1 - 2 * core
    slab_up = jnp.where(slab == NPROJ - 1, 0, slab + 1)
    slab_down = jnp.where(slab == 0, NPROJ - 1, slab - 1)
    slabs = {0: slab, 1: slab_up, -1: slab_down}

    def space_at(step):
        return (me + step) & (NSPACE - 1)

    loads = []
    for i, source in enumerate((design, solid, void)):
        target = raw if i == 0 else masks.at[i - 1]
        loads.append(pltpu.make_async_copy(source, target, in_sem.at[i]))
    for i, source in enumerate((load_in, support_in)):
        for j, step in enumerate((-1, 0, 1)):
            lane = pl.multiple_of(slabs[step] * THICK, THICK)
            loads.append(
                pltpu.make_async_copy(source.at[:, :, pl.ds(lane, THICK)], masks.at[2 + 3 * i + j], in_sem.at[3 + 3 * i + j])
            )
    for item in loads[:3]:
        item.start()

    near = (1, -1, 2, -2)
    halo = [(slabs[e], space_at(d)) for d in near[::-1] + (0,) for e in (1, -1)]
    halo += [(slab, space_at(d)) for d in near]
    rows_y = [(me + (dy << 5)) & 0xE0 for dy in range(NYC)]
    rows_x = [(me + (dx << 3)) & 0x18 for dx in range(NXC)]
    low = me & 0x07
    plane = sorted(
        ((dy, dx) for dy in range(NYC) for dx in range(NXC) if dy or dx),
        key=lambda p: -(min(p[0], NYC - p[0]) + min(p[1], NXC - p[1])),
    )
    plane = [(slab, rows_y[dy] + rows_x[dx] + low) for dy, dx in plane]
    stack = sorted(((dz, dc) for dz in range(NZC) for dc in range(NCORE) if dz or dc), key=lambda p: -min(p[0], NZC - p[0]))
    base = me & 0xF8
    cores = (core, 1 - core)
    levels = []
    for dz in range(NZC):
        z = line_z + dz
        z = jnp.where(z >= NZC, z - NZC, z)
        levels.append((z >> 2, base + ((z & 3) << 1)))
    stack = [(levels[dz][0], levels[dz][1] + cores[dc]) for dz, dc in stack]
    partners = halo + plane + stack

    barrier = pltpu.get_barrier_semaphore()
    for place in partners:
        pl.semaphore_signal(barrier, inc=1, device_id=place, device_id_type=MESH)
    for item in loads[3:]:
        item.start()

    lane = lax.broadcasted_iota(jnp.int32, (1, 128), 1)
    cell_y = lane % WIDTH
    upper = lane >= WIDTH
    has_up = cell_y < WIDTH - 1
    has_down = cell_y > 0

    def y_up(v):
        return jnp.where(has_up, pltpu.roll(v, 127, 1), 0.0)

    def y_down(v):
        return jnp.where(has_down, pltpu.roll(v, 1, 1), 0.0)

    def swap(v):
        return pltpu.roll(v, WIDTH, 1)

    eta = eta_in[0].astype(F32) / 1000.0
    row = lax.broadcasted_iota(jnp.int32, (8, 128), 0)
    tw[slab] = jnp.where(row == 0, eta, weight_in[0])

    for item in loads[:3]:
        item.wait()
    fixed = jnp.where(masks[0] == 1, 1.0, jnp.where(masks[1] == 1, 0.0, raw[...]))
    fb[2, LO:HI, :] = fixed.reshape(128, 128).T

    def remote(source, target, ssem, rsem, place):
        return pltpu.make_async_remote_copy(
            src_ref=source, dst_ref=target, send_sem=ssem, recv_sem=rsem, device_id=place, device_id_type=MESH
        )

    def main_copy(i, source, target, step):
        return remote(
            fb.at[source, pl.ds(LO, THICK), :], fb.at[target, pl.ds(LO, THICK), :],
            send_f.at[i], recv_f.at[i], (slab, space_at(step)),
        )

    from_outer = main_copy(0, 2, 2 + inward, -inward)
    from_far = main_copy(1, 2, 2 - 2 * inward, 2 * inward)
    from_partner = main_copy(2, 2, 2 - inward, inward)
    relay = main_copy(3, 2 - inward, 2 - 2 * inward, inward)
    rims, marks, small = [], [], []
    for i, d in enumerate(near[::-1] + (0,)):
        for j, e in enumerate((1, -1)):
            src, dst = (HI - 8, LO - 8) if e == 1 else (LO, HI)
            rims.append(
                remote(
                    fb.at[2, pl.ds(src, 8), :], fb.at[2 - d, pl.ds(dst, 8), :],
                    send_e.at[2 * i + j], recv_e.at[2 * i + j], (slabs[e], space_at(d)),
                )
            )
    for i, e in enumerate((1, -1)):
        small.append(remote(tw.at[slab], tw.at[slab], send_t.at[i], recv_t.at[i], (slabs[e], me)))

    spill_up = ((me & 7) == 7).astype(jnp.int32)
    spill_down = ((me & 7) == 0).astype(jnp.int32)
    for i, (d, spill) in enumerate(((1, spill_up), (-1, -spill_down))):
        start = pl.multiple_of(THICK + THICK * spill, 8)
        place = jnp.where(spill == 0, slab, slabs[d])
        marks.append(
            remote(
                lt.at[:, pl.ds(start, THICK + 16), :], ls.at[i, :, pl.ds(LO - 8, THICK + 16), :],
                send_m.at[i], recv_m.at[i], (place, space_at(d)),
            )
        )

    pl.semaphore_wait(barrier, len(partners))
    for item in rims[:8] + [from_outer, from_far, from_partner] + rims[8:] + small:
        item.start()

    for item in loads[3:]:
        item.wait()
    for i in range(2):
        for j in range(3):
            turned = masks[2 + 3 * i + j].reshape(128, 128).astype(F32).T
            lt[i, 8 + THICK * j : 8 + THICK * (j + 1), :] = turned
            if j == 0:
                lt[i, 8 + 3 * THICK :, :] = turned[:8, :]
            if j == 2:
                lt[i, 0:8, :] = turned[120:, :]
    for item in marks:
        item.start()

    count_y = has_up.astype(F32) + has_down.astype(F32)
    for k in range(5):
        layer = jnp.where(upper, 1 + k, -k) + me * DEPTH
        in_x = ((layer >= 0) & (layer < GX)).astype(F32)
        count_x = (layer > 0).astype(F32) + (layer < GX - 1).astype(F32)
        for r0, n in ALL:
            z = slab * THICK + (r0 - LO) + lax.broadcasted_iota(jnp.int32, (n, 128), 0)
            in_z = ((z >= 0) & (z < GZ)).astype(F32)
            inm[k, r0 : r0 + n, :] = in_z * in_x
            if k < 4:
                count_z = (z > 0).astype(F32) + (z < GZ - 1).astype(F32)
                pair = count_y * count_z
                total = 2.0 + count_x + count_y + count_z
                total = total + EDGE * (count_x * (count_y + count_z) + pair) + CORNER * (count_x * pair)
                inv[k, r0 : r0 + n, :] = BETA / total

    from_outer.wait_recv()
    relay.start()
    for item in [from_partner, from_far] + small:
        item.wait_recv()
    relay.wait_recv()

    def form_rings(chunks):
        for r0, n in chunks:
            rows = slice(r0, r0 + n)
            ring[0, rows, :] = fb[2, rows, :] * inm[0, rows, :]
            p1, m1, p2, m2 = fb[3, rows, :], fb[1, rows, :], fb[4, rows, :], fb[0, rows, :]
            ring[1, rows, :] = swap(jnp.where(upper, m1, p1)) * inm[1, rows, :]
            ring[2, rows, :] = jnp.where(upper, p1, m1) * inm[2, rows, :]
            ring[3, rows, :] = swap(jnp.where(upper, m2, p2)) * inm[3, rows, :]
            ring[4, rows, :] = jnp.where(upper, p2, m2) * inm[4, rows, :]

    form_rings(OWN)

    etas, tops, scales, weights = [], [], [], []
    for g in range(NPROJ):
        e = tw[g, 0:1, :]
        t = jnp.tanh(BETA * e)
        bottom = t + jnp.tanh(BETA * (1.0 - e))
        etas.append(BETA * e)
        tops.append(t / bottom)
        scales.append(1.0 / bottom)
        weights.append(tw[g, 1:2, :] * (-0.5 * 3.0 * (1.0 - EMIN) * BETA) / bottom)

    def project(chunks):
        for r0, n in chunks:
            rows = slice(r0, r0 + n)
            centre, side = [], []
            for k in range(5):
                v = ring[k, rows, :]
                zb = ring[k, r0 + 1 : r0 + n + 1, :] + ring[k, r0 - 1 : r0 + n - 1, :]
                yb = y_up(v) + y_down(v)
                cross = y_up(zb) + y_down(zb)
                faces = zb + yb
                if k < 4:
                    centre.append(2.0 * v + faces + EDGE * cross)
                side.append(v + EDGE * faces + CORNER * cross)
            for k in range(4):
                inner = side[k - 1] if k else swap(side[0])
                f8 = (centre[k] + (inner + side[k + 1])) * inv[k, rows, :]
                mask = inm[k, rows, :]
                for g in range(NPROJ):
                    t = jnp.tanh(f8 - etas[g])
                    value = t * scales[g] + tops[g]
                    square = value * value
                    hh[g, k, rows, :] = ((0.5 * (1.0 - EMIN)) * (square * value) + 0.5 * EMIN) * mask
                    if k == 0:
                        kk[g, rows, :] = (weights[g] * square) * (1.0 - t * t)

    def precondition(chunks):
        for g in range(NPROJ):
            for k in range(3):
                for r0, n in chunks:
                    rows = slice(r0, r0 + n)
                    h = hh[g, k, rows, :]
                    inner = hh[g, k - 1, rows, :] if k else swap(h)
                    links = [
                        h + inner,
                        h + hh[g, k + 1, rows, :],
                        h + y_up(h),
                        h + y_down(h),
                        h + hh[g, k, r0 + 1 : r0 + n + 1, :],
                        h + hh[g, k, r0 - 1 : r0 + n - 1, :],
                    ]
                    diag = sr[k, rows, :]
                    for i, link in enumerate(links):
                        diag = diag + link
                        if k < 2:
                            cond[g, k, i, rows, :] = link
                    inverse = inm[k, rows, :] / diag
                    zz[g, k, rows, :] = lr[k, rows, :] * inverse
                    if k < 2:
                        idg[g, k, rows, :] = inverse

    def others(field, g, k, r0, n, v):
        rows = slice(r0, r0 + n)
        return [
            field[g, k - 1, rows, :] if k else swap(v),
            field[g, k + 1, rows, :],
            y_up(v),
            y_down(v),
            field[g, k, r0 + 1 : r0 + n + 1, :],
            field[g, k, r0 - 1 : r0 + n - 1, :],
        ]

    def operate(field, g, k, r0, n):
        v = field[g, k, r0 : r0 + n, :]
        total = None
        for i, other in enumerate(others(field, g, k, r0, n, v)):
            term = cond[g, k, i, r0 : r0 + n, :] * (v - other)
            total = term if total is None else total + term
        return v, total

    sums = [[None] * 4 for _ in range(NPROJ)]

    def add(g, i, r0, n, v):
        v = v[max(LO - r0, 0) : n - max(r0 + n - HI, 0)]
        v = jnp.sum(v.reshape(v.shape[0] // 8, 8, 128), axis=0)
        sums[g][i] = v if sums[g][i] is None else sums[g][i] + v

    def first_step(chunks):
        for g in range(NPROJ):
            for k in range(2):
                for r0, n in chunks:
                    rows = slice(r0, r0 + n)
                    v, image = operate(zz, g, k, r0, n)
                    w = image * idg[g, k, rows, :]
                    ww[g, k, rows, :] = w
                    if k == 0:
                        add(g, 0, r0, n, v * lr[0, rows, :])
                        add(g, 1, r0, n, v * image)
                        add(g, 2, r0, n, w * image)

    def second_step(chunks):
        for g in range(NPROJ):
            for r0, n in chunks:
                w, image = operate(ww, g, 0, r0, n)
                add(g, 3, r0, n, w * image)

    project(FILTER[0])

    for item in marks:
        item.wait_recv()

    for r0, n in ALL:
        rows = slice(r0, r0 + n)
        for k in range(3):
            mask = inm[k, rows, :]
            both = []
            for i in range(2):
                if k == 0:
                    both.append(lt[i, r0 + 8 + THICK - LO : r0 + n + 8 + THICK - LO, :])
                elif k == 1:
                    both.append(swap(jnp.where(upper, ls[0, i, rows, :], ls[1, i, rows, :])))
                else:
                    both.append(jnp.where(upper, ls[1, i, rows, :], ls[0, i, rows, :]))
            lr[k, rows, :] = both[0] * mask
            sr[k, rows, :] = PENALTY * jnp.maximum(both[1], 1.0 - mask)

    precondition(DIAGONAL[0])
    first_step(FIRST[0])
    second_step(SECOND[0])

    for item in rims:
        item.wait_recv()
    form_rings(RIM)
    project(FILTER[1])
    precondition(DIAGONAL[1])
    first_step(FIRST[1])
    second_step(SECOND[1])

    parts = jnp.concatenate([jnp.sum(sums[g][i], axis=0, keepdims=True) for i in range(4) for g in range(NPROJ)] + [jnp.zeros((4, 128), F32)], axis=0)
    totals = jnp.sum(parts, axis=1, keepdims=True)
    which = lax.broadcasted_iota(jnp.int32, (16, 128), 0)
    place = (which // NPROJ) * 32 + which % NPROJ
    spot = lax.broadcasted_iota(jnp.int32, (16, 128), 1)
    line = jnp.sum(jnp.where((spot == place) & (which < 12), totals, 0.0), axis=0, keepdims=True)

    def share(value, rows_ref, ssem, rsem, places):
        rows_ref[0] = value
        for d, place in enumerate(places):
            remote(rows_ref.at[0], rows_ref.at[d + 1], ssem.at[0], rsem.at[0], place).start()
        every = rows_ref.at[pl.ds(1, len(places))]
        return remote(every, every, ssem.at[0], rsem.at[0], places[0])

    def gathered(rows_ref, size):
        terms = [rows_ref[d] for d in range(size)]
        while len(terms) > 1:
            terms = [a + b for a, b in zip(terms[::2], terms[1::2])] + terms[len(terms) // 2 * 2 :]
        return terms[0]

    in_plane = share(line, rowp, send_p, recv_p, plane)
    for item in [from_outer, from_far, from_partner, relay] + rims + small + marks:
        item.wait_send()

    for g in range(NPROJ):
        for r0, n in OWN:
            rows = slice(r0, r0 + n)
            v, w = zz[g, 0, rows, :], ww[g, 0, rows, :]
            forms = [None] * 3
            for a, b in zip(others(zz, g, 0, r0, n, v), others(ww, g, 0, r0, n, w)):
                gap_v, gap_w = v - a, w - b
                for i, term in enumerate((gap_v * gap_v, gap_v * gap_w, gap_w * gap_w)):
                    forms[i] = term if forms[i] is None else forms[i] + term
            for i in range(3):
                ee[g, i, r0 - LO : r0 - LO + n, :] = forms[i] * kk[g, rows, :]
        for i in range(3):
            turned_e[g, i] = ee[g, i].T

    in_plane.wait_recv()
    in_stack = share(gathered(rowp, NXC * NYC), rowz, send_z, recv_z, stack)
    in_plane.wait_send()
    in_stack.wait_recv()
    line = gathered(rowz, NZC * NCORE)

    rz0, pq1 = line, pltpu.roll(line, 96, 1)
    qdq, wsw = pltpu.roll(line, 64, 1), pltpu.roll(line, 32, 1)
    step_one = rz0 / pq1
    rz1 = rz0 - 2.0 * step_one * pq1 + step_one * step_one * qdq
    grow = 1.0 + rz1 / rz0
    pq2 = grow * grow * pq1 - 2.0 * grow * step_one * qdq + step_one * step_one * wsw
    step_two = rz1 / pq2
    along = step_one + step_two * grow
    across = -step_one * step_two

    scale = (along * along, 2.0 * along * across, across * across)
    factors = [[jnp.broadcast_to(part[:, g : g + 1], (1, 128)) for part in scale] for g in range(NPROJ)]
    for layer in range(DEPTH):
        for y in range(0, WIDTH, 32):
            rows = slice(layer * WIDTH + y, layer * WIDTH + y + 32)
            result = None
            for g in range(NPROJ):
                for i in range(3):
                    term = factors[g][i] * turned_e[g, i, rows, :]
                    result = term if result is None else result + term
            out[layer, y : y + 32, :] = result

    in_stack.wait_send()


def local(design, solid_mask, void_mask, load_mask, support_mask, thresholds, group_weight):
    dma = pltpu.SemaphoreType.DMA
    return pl.pallas_call(
        kernel,
        out_shape=pltpu.VMEM((DEPTH, WIDTH, THICK), F32),
        in_specs=[pl.BlockSpec(memory_space=pl.ANY)] * 5 + [pl.BlockSpec(memory_space=pltpu.SMEM)] * 2,
        out_specs=pl.BlockSpec(memory_space=pltpu.VMEM),
        scratch_shapes=[
            pltpu.VMEM((DEPTH, WIDTH, THICK), F32),
            pltpu.VMEM((8, DEPTH, WIDTH, THICK), jnp.int32),
            pltpu.VMEM((5, ROWS, 128), F32),
            pltpu.VMEM((2, 3 * THICK + 16, 128), F32),
            pltpu.VMEM((2, 2, ROWS, 128), F32),
            pltpu.VMEM((5, ROWS, 128), F32),
            pltpu.VMEM((3, ROWS, 128), F32),
            pltpu.VMEM((3, ROWS, 128), F32),
            pltpu.VMEM((5, ROWS, 128), F32),
            pltpu.VMEM((4, ROWS, 128), F32),
            pltpu.VMEM((NPROJ, 8, 128), F32),
            pltpu.VMEM((NPROJ, 4, ROWS, 128), F32),
            pltpu.VMEM((NPROJ, 2, 6, ROWS, 128), F32),
            pltpu.VMEM((NPROJ, 3, ROWS, 128), F32),
            pltpu.VMEM((NPROJ, 2, ROWS, 128), F32),
            pltpu.VMEM((NPROJ, 2, ROWS, 128), F32),
            pltpu.VMEM((NPROJ, ROWS, 128), F32),
            pltpu.VMEM((NXC * NYC, 1, 128), F32),
            pltpu.VMEM((NZC * NCORE, 1, 128), F32),
            pltpu.VMEM((NPROJ, 3, THICK, 128), F32),
            pltpu.VMEM((NPROJ, 3, THICK, 128), F32),
            dma((9,)),
            dma((4,)), dma((4,)),
            dma((10,)), dma((10,)),
            dma((2,)), dma((2,)),
            dma((2,)), dma((2,)),
            dma((1,)), dma((1,)),
            dma((1,)), dma((1,)),
        ],
        compiler_params=pltpu.CompilerParams(collective_id=0, has_side_effects=True),
    )(design, solid_mask, void_mask, load_mask, support_mask, thresholds, group_weight)


def solution(mesh):
    placed = (
        P("space", None, "proj"),
        P("space", None, "proj"),
        P("space", None, "proj"),
        P("space", None, None),
        P("space", None, None),
        P("proj"),
        P("proj"),
    )
    return jax.shard_map(
        local, mesh=mesh, in_specs=placed, out_specs=P("space", None, "proj"), check_vma=False
    )
```

```python
import math

import jax
import jax.numpy as jnp
from jax import lax
from jax.experimental import pallas as pl
from jax.experimental.pallas import tpu as pltpu
from jax.sharding import PartitionSpec as P

RMIN = 2.0
BETA = 8.0
EMIN = 0.05
PENALTY = 4.0
MESH = pl.DeviceIdType.MESH
F32 = jnp.float32

NPROJ, NSPACE = 3, 256
NYC, NXC, NZLO, NCORE = 8, 4, 4, 2
NZC = NPROJ * NZLO
DEPTH, WIDTH, THICK = 2, 64, 128
GX, GZ = NSPACE * DEPTH, NPROJ * THICK

LO, HI = 16, 16 + THICK
ROWS = HI + 16
EDGE = 2.0 - math.sqrt(2.0)
CORNER = 2.0 - math.sqrt(3.0)
OWN = [(LO + i, 32) for i in range(0, THICK, 32)]
ALL = [(LO - 8, 8)] + OWN + [(HI, 8)]
REACH = 4
FILTER = [(24, 40), (64, 40), (104, 32)], [(8, 16), (136, 16)]
DIAGONAL = [(32, 32), (64, 32), (96, 32)], [(8, 24), (128, 24)]
FIRST = [(40, 40), (80, 40)], [(8, 32), (120, 32)]
SECOND = [(48, 32), (80, 32)], [(16, 32), (112, 32)]


def kernel(
    design, solid, void, load_in, support_in, eta_in, weight_in, out,
    raw, masks, fb, rim_out, rim_in, lt, ls, ring, lr, sr, inm, inv, tw, hh, cond, zz, idg, ww, kk, rowp, rowz, ee, turned_e,
    eta_held, weight_held,
    in_sem, mask_sem, send_f, recv_f, send_e, recv_e, send_m, recv_m, send_t, recv_t,
    send_p, recv_p, send_z, recv_z,
):
    me = lax.axis_index("space")
    slab = lax.axis_index("proj")
    core = me & 1
    zlo = (me >> 1) & 3
    line_z = slab * NZLO + zlo
    inward = 1 - 2 * core
    slab_up = jnp.where(slab == NPROJ - 1, 0, slab + 1)
    slab_down = jnp.where(slab == 0, NPROJ - 1, slab - 1)
    slabs = {0: slab, 1: slab_up, -1: slab_down}

    def space_at(step):
        return (me + step) & (NSPACE - 1)

    loads = []
    for i, source in enumerate((design, solid, void)):
        target = raw if i == 0 else masks.at[i - 1]
        loads.append(pltpu.make_async_copy(source, target, in_sem.at[i]))
    for i, source in enumerate((load_in, support_in)):
        for j, step in enumerate((-1, 0, 1)):
            lane = pl.multiple_of(slabs[step] * THICK, THICK)
            loads.append(
                pltpu.make_async_copy(source.at[:, :, pl.ds(lane, THICK)], masks.at[2 + 3 * i + j], mask_sem.at[0])
            )
    loads.append(pltpu.make_async_copy(eta_in, eta_held, in_sem.at[3]))
    loads.append(pltpu.make_async_copy(weight_in, weight_held, in_sem.at[4]))
    mask_loads = pltpu.make_async_copy(masks.at[pl.ds(2, 6)], masks.at[pl.ds(2, 6)], mask_sem.at[0])
    for item in loads[:3]:
        item.start()

    near = (1, -1, 2, -2)
    halo = [(slabs[e], space_at(d)) for d in near[::-1] + (0,) for e in (1, -1)]
    halo += [(slab, space_at(d)) for d in near]
    barrier = pltpu.get_barrier_semaphore()
    for place in halo:
        pl.semaphore_signal(barrier, inc=1, device_id=place, device_id_type=MESH)
    for item in loads[9:]:
        item.start()
    rows_y = [(me + (dy << 5)) & 0xE0 for dy in range(NYC)]
    rows_x = [(me + (dx << 3)) & 0x18 for dx in range(NXC)]
    low = me & 0x07
    plane = sorted(
        ((dy, dx) for dy in range(NYC) for dx in range(NXC) if dy or dx),
        key=lambda p: -(min(p[0], NYC - p[0]) + min(p[1], NXC - p[1])),
    )
    plane = [(slab, rows_y[dy] + rows_x[dx] + low) for dy, dx in plane]
    stack = sorted(((dz, dc) for dz in range(NZC) for dc in range(NCORE) if dz or dc), key=lambda p: -min(p[0], NZC - p[0]))
    base = me & 0xF8
    cores = (core, 1 - core)
    levels = []
    for dz in range(NZC):
        z = line_z + dz
        z = jnp.where(z >= NZC, z - NZC, z)
        levels.append((z >> 2, base + ((z & 3) << 1)))
    stack = [(levels[dz][0], levels[dz][1] + cores[dc]) for dz, dc in stack]
    for place in plane + stack:
        pl.semaphore_signal(barrier, inc=1, device_id=place, device_id_type=MESH)
    for item in loads[3:9]:
        item.start()

    lane = lax.broadcasted_iota(jnp.int32, (1, 128), 1)
    cell_y = lane % WIDTH
    upper = lane >= WIDTH
    has_up = cell_y < WIDTH - 1
    has_down = cell_y > 0

    def y_up(v):
        return jnp.where(has_up, pltpu.roll(v, 127, 1), 0.0)

    def y_down(v):
        return jnp.where(has_down, pltpu.roll(v, 1, 1), 0.0)

    def swap(v):
        return pltpu.roll(v, WIDTH, 1)

    for item in loads[:3]:
        item.wait()
    fixed = jnp.where(masks[0] == 1, 1.0, jnp.where(masks[1] == 1, 0.0, raw[...])).reshape(128, 128).T
    fb[2, LO:HI, :] = fixed
    rim_out[0] = fixed[THICK - REACH :, :]
    rim_out[1] = fixed[:REACH, :]

    for item in loads[9:]:
        item.wait()
    eta = eta_held[0, 0].astype(F32) / 1000.0
    row = lax.broadcasted_iota(jnp.int32, (8, 128), 0)
    tw[slab] = jnp.where(row == 0, eta, weight_held[0, 0])

    def remote(source, target, ssem, rsem, place):
        return pltpu.make_async_remote_copy(
            src_ref=source, dst_ref=target, send_sem=ssem, recv_sem=rsem, device_id=place, device_id_type=MESH
        )

    def main_copy(i, source, target, step):
        return remote(
            fb.at[source, pl.ds(LO, THICK), :], fb.at[target, pl.ds(LO, THICK), :],
            send_f.at[0], recv_f.at[i], (slab, space_at(step)),
        )

    from_outer = main_copy(0, 2, 2 + inward, -inward)
    from_far = main_copy(1, 2, 2 - 2 * inward, 2 * inward)
    from_partner = main_copy(2, 2, 2 - inward, inward)
    relay = main_copy(3, 2 - inward, 2 - 2 * inward, inward)
    rims, marks, small = [], [], []
    for d in near[::-1] + (0,):
        for j, e in enumerate((1, -1)):
            rims.append(remote(rim_out.at[j], rim_in.at[2 - d, j], send_e.at[0], recv_e.at[0], (slabs[e], space_at(d))))
    for i, e in enumerate((1, -1)):
        small.append(remote(tw.at[slab], tw.at[slab], send_t.at[0], recv_t.at[0], (slabs[e], me)))

    spill_up = ((me & 7) == 7).astype(jnp.int32)
    spill_down = ((me & 7) == 0).astype(jnp.int32)
    for i, (d, spill) in enumerate(((1, spill_up), (-1, -spill_down))):
        start = pl.multiple_of(THICK + THICK * spill, 8)
        place = jnp.where(spill == 0, slab, slabs[d])
        marks.append(
            remote(
                lt.at[:, pl.ds(start, THICK + 16), :], ls.at[i, :, pl.ds(LO - 8, THICK + 16), :],
                send_m.at[0], recv_m.at[0], (place, space_at(d)),
            )
        )

    def whole(ref, ssem, rsem):
        return remote(ref, ref, ssem.at[0], rsem.at[0], (slab, space_at(1)))

    all_main = whole(fb.at[pl.ds(0, 4), pl.ds(LO, THICK), :], send_f, recv_f)
    all_rims = whole(rim_in, send_e, recv_e)
    all_marks = whole(ls.at[:, :, pl.ds(LO - 8, THICK + 16), :], send_m, recv_m)
    all_small = whole(tw.at[pl.ds(0, 2)], send_t, recv_t)

    pl.semaphore_wait(barrier, len(halo) + len(plane) + len(stack))
    for item in rims[:8] + [from_outer, from_far, from_partner] + rims[8:] + small:
        item.start()

    mask_loads.wait()
    for i in range(2):
        for j in range(3):
            turned = masks[2 + 3 * i + j].reshape(128, 128).astype(F32).T
            lt[i, 8 + THICK * j : 8 + THICK * (j + 1), :] = turned
            if j == 0:
                lt[i, 8 + 3 * THICK :, :] = turned[:8, :]
            if j == 2:
                lt[i, 0:8, :] = turned[120:, :]
    for item in marks:
        item.start()

    count_y = has_up.astype(F32) + has_down.astype(F32)
    for k in range(5):
        layer = jnp.where(upper, 1 + k, -k) + me * DEPTH
        in_x = ((layer >= 0) & (layer < GX)).astype(F32)
        count_x = (layer > 0).astype(F32) + (layer < GX - 1).astype(F32)
        for r0, n in ALL:
            z = slab * THICK + (r0 - LO) + lax.broadcasted_iota(jnp.int32, (n, 128), 0)
            in_z = ((z >= 0) & (z < GZ)).astype(F32)
            inm[k, r0 : r0 + n, :] = in_z * in_x
            if k < 4:
                count_z = (z > 0).astype(F32) + (z < GZ - 1).astype(F32)
                pair = count_y * count_z
                total = 2.0 + count_x + count_y + count_z
                total = total + EDGE * (count_x * (count_y + count_z) + pair) + CORNER * (count_x * pair)
                inv[k, r0 : r0 + n, :] = BETA / total

    from_outer.wait_recv()
    relay.start()
    for item in (from_partner, from_far, all_small, relay):
        item.wait_recv()

    def form_rings(r0, n, bricks):
        rows = slice(r0, r0 + n)
        m2, m1, own, p1, p2 = bricks
        ring[0, rows, :] = own * inm[0, rows, :]
        ring[1, rows, :] = swap(jnp.where(upper, m1, p1)) * inm[1, rows, :]
        ring[2, rows, :] = jnp.where(upper, p1, m1) * inm[2, rows, :]
        ring[3, rows, :] = swap(jnp.where(upper, m2, p2)) * inm[3, rows, :]
        ring[4, rows, :] = jnp.where(upper, p2, m2) * inm[4, rows, :]

    for r0, n in OWN:
        form_rings(r0, n, [fb[i, r0 : r0 + n, :] for i in range(5)])

    etas, tops, scales, weights = [], [], [], []
    for g in range(NPROJ):
        e = tw[g, 0:1, :]
        t = jnp.tanh(BETA * e)
        bottom = t + jnp.tanh(BETA * (1.0 - e))
        etas.append(BETA * e)
        tops.append(t / bottom)
        scales.append(1.0 / bottom)
        weights.append(tw[g, 1:2, :] * (-0.5 * 3.0 * (1.0 - EMIN) * BETA) / bottom)

    def project(chunks):
        for r0, n in chunks:
            rows = slice(r0, r0 + n)
            centre, side = [], []
            for k in range(5):
                v = ring[k, rows, :]
                zb = ring[k, r0 + 1 : r0 + n + 1, :] + ring[k, r0 - 1 : r0 + n - 1, :]
                yb = y_up(v) + y_down(v)
                cross = y_up(zb) + y_down(zb)
                faces = zb + yb
                if k < 4:
                    centre.append(2.0 * v + faces + EDGE * cross)
                side.append(v + EDGE * faces + CORNER * cross)
            for k in range(4):
                inner = side[k - 1] if k else swap(side[0])
                f8 = (centre[k] + (inner + side[k + 1])) * inv[k, rows, :]
                mask = inm[k, rows, :]
                for g in range(NPROJ):
                    t = jnp.tanh(f8 - etas[g])
                    value = t * scales[g] + tops[g]
                    square = value * value
                    hh[g, k, rows, :] = ((0.5 * (1.0 - EMIN)) * (square * value) + 0.5 * EMIN) * mask
                    if k == 0:
                        kk[g, rows, :] = (weights[g] * square) * (1.0 - t * t)

    def precondition(chunks):
        for g in range(NPROJ):
            for k in range(3):
                for r0, n in chunks:
                    rows = slice(r0, r0 + n)
                    h = hh[g, k, rows, :]
                    inner = hh[g, k - 1, rows, :] if k else swap(h)
                    links = [
                        h + inner,
                        h + hh[g, k + 1, rows, :],
                        h + y_up(h),
                        h + y_down(h),
                        h + hh[g, k, r0 + 1 : r0 + n + 1, :],
                        h + hh[g, k, r0 - 1 : r0 + n - 1, :],
                    ]
                    diag = sr[k, rows, :]
                    for i, link in enumerate(links):
                        diag = diag + link
                        if k < 2:
                            cond[g, k, i, rows, :] = link
                    inverse = inm[k, rows, :] / diag
                    zz[g, k, rows, :] = lr[k, rows, :] * inverse
                    if k < 2:
                        idg[g, k, rows, :] = inverse

    def others(field, g, k, r0, n, v):
        rows = slice(r0, r0 + n)
        return [
            field[g, k - 1, rows, :] if k else swap(v),
            field[g, k + 1, rows, :],
            y_up(v),
            y_down(v),
            field[g, k, r0 + 1 : r0 + n + 1, :],
            field[g, k, r0 - 1 : r0 + n - 1, :],
        ]

    def operate(field, g, k, r0, n):
        v = field[g, k, r0 : r0 + n, :]
        total = None
        for i, other in enumerate(others(field, g, k, r0, n, v)):
            term = cond[g, k, i, r0 : r0 + n, :] * (v - other)
            total = term if total is None else total + term
        return v, total

    sums = [[None] * 4 for _ in range(NPROJ)]

    def add(g, i, r0, n, v):
        v = v[max(LO - r0, 0) : n - max(r0 + n - HI, 0)]
        v = jnp.sum(v.reshape(v.shape[0] // 8, 8, 128), axis=0)
        sums[g][i] = v if sums[g][i] is None else sums[g][i] + v

    def first_step(chunks):
        for g in range(NPROJ):
            for k in range(2):
                for r0, n in chunks:
                    rows = slice(r0, r0 + n)
                    v, image = operate(zz, g, k, r0, n)
                    w = image * idg[g, k, rows, :]
                    ww[g, k, rows, :] = w
                    if k == 0:
                        add(g, 0, r0, n, v * lr[0, rows, :])
                        add(g, 1, r0, n, v * image)
                        add(g, 2, r0, n, w * image)

    def second_step(chunks):
        for g in range(NPROJ):
            for r0, n in chunks:
                w, image = operate(ww, g, 0, r0, n)
                add(g, 3, r0, n, w * image)

    project(FILTER[0])

    all_marks.wait_recv()

    for r0, n in ALL:
        rows = slice(r0, r0 + n)
        for k in range(3):
            mask = inm[k, rows, :]
            both = []
            for i in range(2):
                if k == 0:
                    both.append(lt[i, r0 + 8 + THICK - LO : r0 + n + 8 + THICK - LO, :])
                elif k == 1:
                    both.append(swap(jnp.where(upper, ls[0, i, rows, :], ls[1, i, rows, :])))
                else:
                    both.append(jnp.where(upper, ls[1, i, rows, :], ls[0, i, rows, :]))
            lr[k, rows, :] = both[0] * mask
            sr[k, rows, :] = PENALTY * jnp.maximum(both[1], 1.0 - mask)

    precondition(DIAGONAL[0])
    first_step(FIRST[0])
    second_step(SECOND[0])

    all_rims.wait_recv()
    for j, r0 in enumerate((LO - REACH, HI)):
        form_rings(r0, REACH, [rim_in[i, j] for i in range(5)])
    project(FILTER[1])
    precondition(DIAGONAL[1])
    first_step(FIRST[1])
    second_step(SECOND[1])

    parts = jnp.concatenate([jnp.sum(sums[g][i], axis=0, keepdims=True) for i in range(4) for g in range(NPROJ)] + [jnp.zeros((4, 128), F32)], axis=0)
    totals = jnp.sum(parts, axis=1, keepdims=True)
    which = lax.broadcasted_iota(jnp.int32, (16, 128), 0)
    place = (which // NPROJ) * 32 + which % NPROJ
    spot = lax.broadcasted_iota(jnp.int32, (16, 128), 1)
    line = jnp.sum(jnp.where((spot == place) & (which < 12), totals, 0.0), axis=0, keepdims=True)

    def share(value, rows_ref, ssem, rsem, places):
        rows_ref[0] = value
        for d, place in enumerate(places):
            remote(rows_ref.at[0], rows_ref.at[d + 1], ssem.at[0], rsem.at[0], place).start()
        every = rows_ref.at[pl.ds(1, len(places))]
        return remote(every, every, ssem.at[0], rsem.at[0], places[0])

    def gathered(rows_ref, size):
        terms = [rows_ref[d] for d in range(size)]
        while len(terms) > 1:
            terms = [a + b for a, b in zip(terms[::2], terms[1::2])] + terms[len(terms) // 2 * 2 :]
        return terms[0]

    in_plane = share(line, rowp, send_p, recv_p, plane)
    for item in (all_main, all_rims, all_small, all_marks):
        item.wait_send()

    for g in range(NPROJ):
        for r0, n in OWN:
            rows = slice(r0, r0 + n)
            v, w = zz[g, 0, rows, :], ww[g, 0, rows, :]
            forms = [None] * 3
            for a, b in zip(others(zz, g, 0, r0, n, v), others(ww, g, 0, r0, n, w)):
                gap_v, gap_w = v - a, w - b
                for i, term in enumerate((gap_v * gap_v, gap_v * gap_w, gap_w * gap_w)):
                    forms[i] = term if forms[i] is None else forms[i] + term
            for i in range(3):
                ee[g, i, r0 - LO : r0 - LO + n, :] = forms[i] * kk[g, rows, :]
        for i in range(3):
            turned_e[g, i] = ee[g, i].T

    in_plane.wait_recv()
    in_stack = share(gathered(rowp, NXC * NYC), rowz, send_z, recv_z, stack)
    in_plane.wait_send()
    in_stack.wait_recv()
    line = gathered(rowz, NZC * NCORE)

    rz0, pq1 = line, pltpu.roll(line, 96, 1)
    qdq, wsw = pltpu.roll(line, 64, 1), pltpu.roll(line, 32, 1)
    step_one = rz0 / pq1
    rz1 = rz0 - 2.0 * step_one * pq1 + step_one * step_one * qdq
    grow = 1.0 + rz1 / rz0
    pq2 = grow * grow * pq1 - 2.0 * grow * step_one * qdq + step_one * step_one * wsw
    step_two = rz1 / pq2
    along = step_one + step_two * grow
    across = -step_one * step_two

    scale = (along * along, 2.0 * along * across, across * across)
    factors = [[jnp.broadcast_to(part[:, g : g + 1], (1, 128)) for part in scale] for g in range(NPROJ)]
    for layer in range(DEPTH):
        for y in range(0, WIDTH, 32):
            rows = slice(layer * WIDTH + y, layer * WIDTH + y + 32)
            result = None
            for g in range(NPROJ):
                for i in range(3):
                    term = factors[g][i] * turned_e[g, i, rows, :]
                    result = term if result is None else result + term
            out[layer, y : y + 32, :] = result

    in_stack.wait_send()


def local(design, solid_mask, void_mask, load_mask, support_mask, thresholds, group_weight):
    dma = pltpu.SemaphoreType.DMA
    return pl.pallas_call(
        kernel,
        out_shape=pltpu.VMEM((DEPTH, WIDTH, THICK), F32),
        in_specs=[pl.BlockSpec(memory_space=pl.ANY)] * 5 + [pl.BlockSpec(memory_space=pltpu.HBM)] * 2,
        out_specs=pl.BlockSpec(memory_space=pltpu.VMEM),
        scratch_shapes=[
            pltpu.VMEM((DEPTH, WIDTH, THICK), F32),
            pltpu.VMEM((8, DEPTH, WIDTH, THICK), jnp.int32),
            pltpu.VMEM((5, ROWS, 128), F32),
            pltpu.VMEM((2, REACH, 128), F32),
            pltpu.VMEM((5, 2, REACH, 128), F32),
            pltpu.VMEM((2, 3 * THICK + 16, 128), F32),
            pltpu.VMEM((2, 2, ROWS, 128), F32),
            pltpu.VMEM((5, ROWS, 128), F32),
            pltpu.VMEM((3, ROWS, 128), F32),
            pltpu.VMEM((3, ROWS, 128), F32),
            pltpu.VMEM((5, ROWS, 128), F32),
            pltpu.VMEM((4, ROWS, 128), F32),
            pltpu.VMEM((NPROJ, 8, 128), F32),
            pltpu.VMEM((NPROJ, 4, ROWS, 128), F32),
            pltpu.VMEM((NPROJ, 2, 6, ROWS, 128), F32),
            pltpu.VMEM((NPROJ, 3, ROWS, 128), F32),
            pltpu.VMEM((NPROJ, 2, ROWS, 128), F32),
            pltpu.VMEM((NPROJ, 2, ROWS, 128), F32),
            pltpu.VMEM((NPROJ, ROWS, 128), F32),
            pltpu.VMEM((NXC * NYC, 1, 128), F32),
            pltpu.VMEM((NZC * NCORE, 1, 128), F32),
            pltpu.VMEM((NPROJ, 3, THICK, 128), F32),
            pltpu.VMEM((NPROJ, 3, THICK, 128), F32),
            pltpu.SMEM((1, 1), jnp.int32),
            pltpu.SMEM((1, 1), F32),
            dma((5,)), dma((1,)),
            dma((1,)), dma((4,)),
            dma((1,)), dma((1,)),
            dma((1,)), dma((1,)),
            dma((1,)), dma((1,)),
            dma((1,)), dma((1,)),
            dma((1,)), dma((1,)),
        ],
        compiler_params=pltpu.CompilerParams(collective_id=0, has_side_effects=True),
    )(
        design, solid_mask, void_mask, load_mask, support_mask,
        thresholds.reshape(1, 1), group_weight.reshape(1, 1),
    )


def solution(mesh):
    placed = (
        P("space", None, "proj"),
        P("space", None, "proj"),
        P("space", None, "proj"),
        P("space", None, None),
        P("space", None, None),
        P("proj"),
        P("proj"),
    )
    return jax.shard_map(
        local, mesh=mesh, in_specs=placed, out_specs=P("space", None, "proj"), check_vma=False
    )
```

```python
import math

import jax
import jax.numpy as jnp
from jax import lax
from jax.experimental import pallas as pl
from jax.experimental.pallas import tpu as pltpu
from jax.sharding import PartitionSpec as P

RMIN = 2.0
BETA = 8.0
EMIN = 0.05
PENALTY = 4.0
MESH = pl.DeviceIdType.MESH
F32 = jnp.float32

NPROJ, NSPACE = 3, 256
NYC, NXC, NZLO, NCORE = 8, 4, 4, 2
NZC = NPROJ * NZLO
DEPTH, WIDTH, THICK = 2, 64, 128
GX, GZ = NSPACE * DEPTH, NPROJ * THICK

LO, HI = 16, 16 + THICK
ROWS = HI + 16
EDGE = 2.0 - math.sqrt(2.0)
CORNER = 2.0 - math.sqrt(3.0)
OWN = [(LO + i, 32) for i in range(0, THICK, 32)]
ALL = [(LO - 8, 8)] + OWN + [(HI, 8)]
REACH = 4
FILTER = [(24, 40), (64, 40), (104, 32)], [(8, 16), (136, 16)]
DIAGONAL = [(32, 32), (64, 32), (96, 32)], [(8, 24), (128, 24)]
FIRST = [(40, 40), (80, 40)], [(8, 32), (120, 32)]
SECOND = [(48, 32), (80, 32)], [(16, 32), (112, 32)]


def kernel(
    design, solid, void, load_in, support_in, eta_in, weight_in, out,
    raw, masks, fb, rim_out, rim_in, lt, ls, ring, lr, sr, inm, inv, tw, hh, cond, zz, idg, ww, kk, rowp, rowz, ee, turned_e,
    eta_held, weight_held,
    in_sem, mask_sem, send_f, recv_f, send_e, recv_e, send_m, recv_m, send_t, recv_t,
    send_p, recv_p, send_z, recv_z,
):
    me = lax.axis_index("space")
    slab = lax.axis_index("proj")
    core = me & 1
    zlo = (me >> 1) & 3
    line_z = slab * NZLO + zlo
    inward = 1 - 2 * core
    slab_up = jnp.where(slab == NPROJ - 1, 0, slab + 1)
    slab_down = jnp.where(slab == 0, NPROJ - 1, slab - 1)
    slabs = {0: slab, 1: slab_up, -1: slab_down}

    def space_at(step):
        return (me + step) & (NSPACE - 1)

    loads = []
    for i, source in enumerate((design, solid, void)):
        target = raw if i == 0 else masks.at[i - 1]
        loads.append(pltpu.make_async_copy(source, target, in_sem.at[i]))
    for i, source in enumerate((load_in, support_in)):
        for j, step in enumerate((-1, 0, 1)):
            lane = pl.multiple_of(slabs[step] * THICK, THICK)
            loads.append(
                pltpu.make_async_copy(source.at[:, :, pl.ds(lane, THICK)], masks.at[2 + 3 * i + j], mask_sem.at[0])
            )
    loads.append(pltpu.make_async_copy(eta_in, eta_held, in_sem.at[3]))
    loads.append(pltpu.make_async_copy(weight_in, weight_held, in_sem.at[4]))
    mask_loads = pltpu.make_async_copy(masks.at[pl.ds(2, 6)], masks.at[pl.ds(2, 6)], mask_sem.at[0])
    for item in loads[:3]:
        item.start()

    near = (1, -1, 2, -2)
    halo = [(slabs[e], space_at(d)) for d in near[::-1] + (0,) for e in (1, -1)]
    halo += [(slab, space_at(d)) for d in near]
    barrier = pltpu.get_barrier_semaphore()
    for place in halo:
        pl.semaphore_signal(barrier, inc=1, device_id=place, device_id_type=MESH)
    for item in loads[9:]:
        item.start()
    rows_y = [(me + (dy << 5)) & 0xE0 for dy in range(NYC)]
    rows_x = [(me + (dx << 3)) & 0x18 for dx in range(NXC)]
    low = me & 0x07
    plane = sorted(
        ((dy, dx) for dy in range(NYC) for dx in range(NXC) if dy or dx),
        key=lambda p: -(min(p[0], NYC - p[0]) + min(p[1], NXC - p[1])),
    )
    plane = [(slab, rows_y[dy] + rows_x[dx] + low) for dy, dx in plane]
    stack = sorted(((dz, dc) for dz in range(NZC) for dc in range(NCORE) if dz or dc), key=lambda p: -min(p[0], NZC - p[0]))
    base = me & 0xF8
    cores = (core, 1 - core)
    levels = []
    for dz in range(NZC):
        z = line_z + dz
        z = jnp.where(z >= NZC, z - NZC, z)
        levels.append((z >> 2, base + ((z & 3) << 1)))
    stack = [(levels[dz][0], levels[dz][1] + cores[dc]) for dz, dc in stack]
    for place in plane + stack:
        pl.semaphore_signal(barrier, inc=1, device_id=place, device_id_type=MESH)
    for item in loads[3:9]:
        item.start()

    lane = lax.broadcasted_iota(jnp.int32, (1, 128), 1)
    cell_y = lane % WIDTH
    upper = lane >= WIDTH
    has_up = cell_y < WIDTH - 1
    has_down = cell_y > 0

    def y_up(v):
        return jnp.where(has_up, pltpu.roll(v, 127, 1), 0.0)

    def y_down(v):
        return jnp.where(has_down, pltpu.roll(v, 1, 1), 0.0)

    def swap(v):
        return pltpu.roll(v, WIDTH, 1)

    for item in loads[:3]:
        item.wait()
    fixed = jnp.where(masks[0] == 1, 1.0, jnp.where(masks[1] == 1, 0.0, raw[...])).reshape(128, 128).T
    fb[2, LO:HI, :] = fixed
    rim_out[0] = fixed[THICK - REACH :, :]
    rim_out[1] = fixed[:REACH, :]

    for item in loads[9:]:
        item.wait()
    eta = eta_held[0, 0].astype(F32) / 1000.0
    row = lax.broadcasted_iota(jnp.int32, (8, 128), 0)
    tw[slab] = jnp.where(row == 0, eta, weight_held[0, 0])

    def remote(source, target, ssem, rsem, place):
        return pltpu.make_async_remote_copy(
            src_ref=source, dst_ref=target, send_sem=ssem, recv_sem=rsem, device_id=place, device_id_type=MESH
        )

    def main_copy(i, source, target, step):
        return remote(
            fb.at[source, pl.ds(LO, THICK), :], fb.at[target, pl.ds(LO, THICK), :],
            send_f.at[0], recv_f.at[i], (slab, space_at(step)),
        )

    from_outer = main_copy(0, 2, 2 + inward, -inward)
    from_far = main_copy(1, 2, 2 - 2 * inward, 2 * inward)
    from_partner = main_copy(2, 2, 2 - inward, inward)
    relay = main_copy(3, 2 - inward, 2 - 2 * inward, inward)
    rims, marks, small = [], [], []
    for d in near[::-1] + (0,):
        for j, e in enumerate((1, -1)):
            rims.append(remote(rim_out.at[j], rim_in.at[2 - d, j], send_e.at[0], recv_e.at[0], (slabs[e], space_at(d))))
    for i, e in enumerate((1, -1)):
        small.append(remote(tw.at[slab], tw.at[slab], send_t.at[0], recv_t.at[0], (slabs[e], me)))

    spill_up = ((me & 7) == 7).astype(jnp.int32)
    spill_down = ((me & 7) == 0).astype(jnp.int32)
    for i, (d, spill) in enumerate(((1, spill_up), (-1, -spill_down))):
        start = pl.multiple_of(THICK + THICK * spill, 8)
        place = jnp.where(spill == 0, slab, slabs[d])
        marks.append(
            remote(
                lt.at[:, pl.ds(start, THICK + 16), :], ls.at[i, :, pl.ds(LO - 8, THICK + 16), :],
                send_m.at[0], recv_m.at[0], (place, space_at(d)),
            )
        )

    def whole(ref, ssem, rsem):
        return remote(ref, ref, ssem.at[0], rsem.at[0], (slab, space_at(1)))

    all_main = whole(fb.at[pl.ds(0, 4), pl.ds(LO, THICK), :], send_f, recv_f)
    all_rims = whole(rim_in, send_e, recv_e)
    all_marks = whole(ls.at[:, :, pl.ds(LO - 8, THICK + 16), :], send_m, recv_m)
    all_small = whole(tw.at[pl.ds(0, 2)], send_t, recv_t)

    pl.semaphore_wait(barrier, len(halo) + len(plane) + len(stack))
    for item in rims[:8] + [from_outer, from_partner] + rims[8:] + small:
        item.start()

    mask_loads.wait()
    for i in range(2):
        for j in range(3):
            turned = masks[2 + 3 * i + j].reshape(128, 128).astype(F32).T
            lt[i, 8 + THICK * j : 8 + THICK * (j + 1), :] = turned
            if j == 0:
                lt[i, 8 + 3 * THICK :, :] = turned[:8, :]
            if j == 2:
                lt[i, 0:8, :] = turned[120:, :]

    count_y = has_up.astype(F32) + has_down.astype(F32)
    for k in range(5):
        layer = jnp.where(upper, 1 + k, -k) + me * DEPTH
        in_x = ((layer >= 0) & (layer < GX)).astype(F32)
        count_x = (layer > 0).astype(F32) + (layer < GX - 1).astype(F32)
        for r0, n in ALL:
            z = slab * THICK + (r0 - LO) + lax.broadcasted_iota(jnp.int32, (n, 128), 0)
            in_z = ((z >= 0) & (z < GZ)).astype(F32)
            inm[k, r0 : r0 + n, :] = in_z * in_x
            if k < 4:
                count_z = (z > 0).astype(F32) + (z < GZ - 1).astype(F32)
                pair = count_y * count_z
                total = 2.0 + count_x + count_y + count_z
                total = total + EDGE * (count_x * (count_y + count_z) + pair) + CORNER * (count_x * pair)
                inv[k, r0 : r0 + n, :] = BETA / total

    from_far.start()
    for item in marks:
        item.start()
    from_outer.wait_recv()
    relay.start()
    for item in (from_partner, from_far, all_small, relay):
        item.wait_recv()

    def form_rings(r0, n, bricks):
        rows = slice(r0, r0 + n)
        m2, m1, own, p1, p2 = bricks
        ring[0, rows, :] = own * inm[0, rows, :]
        ring[1, rows, :] = swap(jnp.where(upper, m1, p1)) * inm[1, rows, :]
        ring[2, rows, :] = jnp.where(upper, p1, m1) * inm[2, rows, :]
        ring[3, rows, :] = swap(jnp.where(upper, m2, p2)) * inm[3, rows, :]
        ring[4, rows, :] = jnp.where(upper, p2, m2) * inm[4, rows, :]

    for r0, n in OWN:
        form_rings(r0, n, [fb[i, r0 : r0 + n, :] for i in range(5)])

    etas, tops, scales, weights = [], [], [], []
    for g in range(NPROJ):
        e = tw[g, 0:1, :]
        t = jnp.tanh(BETA * e)
        bottom = t + jnp.tanh(BETA * (1.0 - e))
        etas.append(BETA * e)
        tops.append(t / bottom)
        scales.append(1.0 / bottom)
        weights.append(tw[g, 1:2, :] * (-0.5 * 3.0 * (1.0 - EMIN) * BETA) / bottom)

    def project(chunks):
        for r0, n in chunks:
            rows = slice(r0, r0 + n)
            plain = [ring[k, rows, :] for k in range(5)]
            beside = [ring[k, r0 + 1 : r0 + n + 1, :] + ring[k, r0 - 1 : r0 + n - 1, :] for k in range(5)]
            for k in range(4):
                v, zb = plain[k], beside[k]
                vx = (plain[k - 1] if k else swap(v)) + plain[k + 1]
                zx = (beside[k - 1] if k else swap(zb)) + beside[k + 1]
                line_y = v + EDGE * (zb + vx) + CORNER * zx
                total = 2.0 * v + (zb + vx) + EDGE * zx + (y_up(line_y) + y_down(line_y))
                f8 = total * inv[k, rows, :]
                mask = inm[k, rows, :]
                for g in range(NPROJ):
                    t = jnp.tanh(f8 - etas[g])
                    value = t * scales[g] + tops[g]
                    square = value * value
                    hh[g, k, rows, :] = ((0.5 * (1.0 - EMIN)) * (square * value) + 0.5 * EMIN) * mask
                    if k == 0:
                        kk[g, rows, :] = (weights[g] * square) * (1.0 - t * t)

    def precondition(chunks):
        for g in range(NPROJ):
            for k in range(3):
                for r0, n in chunks:
                    rows = slice(r0, r0 + n)
                    h = hh[g, k, rows, :]
                    inner = hh[g, k - 1, rows, :] if k else swap(h)
                    near_h = [
                        inner,
                        hh[g, k + 1, rows, :],
                        y_up(h),
                        y_down(h),
                        hh[g, k, r0 + 1 : r0 + n + 1, :],
                        hh[g, k, r0 - 1 : r0 + n - 1, :],
                    ]
                    diag = sr[k, rows, :]
                    if k == 2:
                        diag = diag + 6.0 * h
                    for i, other in enumerate(near_h):
                        if k < 2:
                            other = h + other
                            cond[g, k, i, rows, :] = other
                        diag = diag + other
                    inverse = inm[k, rows, :] / diag
                    zz[g, k, rows, :] = lr[k, rows, :] * inverse
                    if k < 2:
                        idg[g, k, rows, :] = inverse

    def others(field, g, k, r0, n, v):
        rows = slice(r0, r0 + n)
        return [
            field[g, k - 1, rows, :] if k else swap(v),
            field[g, k + 1, rows, :],
            y_up(v),
            y_down(v),
            field[g, k, r0 + 1 : r0 + n + 1, :],
            field[g, k, r0 - 1 : r0 + n - 1, :],
        ]

    def operate(field, g, k, r0, n):
        v = field[g, k, r0 : r0 + n, :]
        total = None
        for i, other in enumerate(others(field, g, k, r0, n, v)):
            term = cond[g, k, i, r0 : r0 + n, :] * (v - other)
            total = term if total is None else total + term
        return v, total

    sums = [[None] * 4 for _ in range(NPROJ)]

    def add(g, i, r0, n, v):
        v = v[max(LO - r0, 0) : n - max(r0 + n - HI, 0)]
        v = jnp.sum(v.reshape(v.shape[0] // 8, 8, 128), axis=0)
        sums[g][i] = v if sums[g][i] is None else sums[g][i] + v

    def first_step(chunks):
        for g in range(NPROJ):
            for k in range(2):
                for r0, n in chunks:
                    rows = slice(r0, r0 + n)
                    v, image = operate(zz, g, k, r0, n)
                    w = image * idg[g, k, rows, :]
                    ww[g, k, rows, :] = w
                    if k == 0:
                        add(g, 0, r0, n, v * lr[0, rows, :])
                        add(g, 1, r0, n, v * image)
                        add(g, 2, r0, n, w * image)

    def second_step(chunks):
        for g in range(NPROJ):
            for r0, n in chunks:
                w, image = operate(ww, g, 0, r0, n)
                add(g, 3, r0, n, w * image)

    project(FILTER[0])

    all_marks.wait_recv()

    for r0, n in ALL:
        rows = slice(r0, r0 + n)
        for k in range(3):
            mask = inm[k, rows, :]
            both = []
            for i in range(2):
                if k == 0:
                    both.append(lt[i, r0 + 8 + THICK - LO : r0 + n + 8 + THICK - LO, :])
                elif k == 1:
                    both.append(swap(jnp.where(upper, ls[0, i, rows, :], ls[1, i, rows, :])))
                else:
                    both.append(jnp.where(upper, ls[1, i, rows, :], ls[0, i, rows, :]))
            lr[k, rows, :] = both[0] * mask
            sr[k, rows, :] = PENALTY * jnp.maximum(both[1], 1.0 - mask)

    precondition(DIAGONAL[0])
    first_step(FIRST[0])
    second_step(SECOND[0])

    all_rims.wait_recv()
    for j, r0 in enumerate((LO - REACH, HI)):
        form_rings(r0, REACH, [rim_in[i, j] for i in range(5)])
    project(FILTER[1])
    precondition(DIAGONAL[1])
    first_step(FIRST[1])
    second_step(SECOND[1])

    parts = jnp.concatenate([jnp.sum(sums[g][i], axis=0, keepdims=True) for i in range(4) for g in range(NPROJ)] + [jnp.zeros((4, 128), F32)], axis=0)
    totals = jnp.sum(parts, axis=1, keepdims=True)
    which = lax.broadcasted_iota(jnp.int32, (16, 128), 0)
    place = (which // NPROJ) * 32 + which % NPROJ
    spot = lax.broadcasted_iota(jnp.int32, (16, 128), 1)
    line = jnp.sum(jnp.where((spot == place) & (which < 12), totals, 0.0), axis=0, keepdims=True)

    def share(value, rows_ref, ssem, rsem, places):
        rows_ref[0] = value
        for d, place in enumerate(places):
            remote(rows_ref.at[0], rows_ref.at[d + 1], ssem.at[0], rsem.at[0], place).start()
        every = rows_ref.at[pl.ds(1, len(places))]
        return remote(every, every, ssem.at[0], rsem.at[0], places[0])

    def gathered(rows_ref, size):
        terms = [rows_ref[d] for d in range(size)]
        while len(terms) > 1:
            terms = [a + b for a, b in zip(terms[::2], terms[1::2])] + terms[len(terms) // 2 * 2 :]
        return terms[0]

    in_plane = share(line, rowp, send_p, recv_p, plane)
    for item in (all_main, all_rims, all_small, all_marks):
        item.wait_send()

    for g in range(NPROJ):
        for r0, n in OWN:
            rows = slice(r0, r0 + n)
            v, w = zz[g, 0, rows, :], ww[g, 0, rows, :]
            forms = [None] * 3
            for a, b in zip(others(zz, g, 0, r0, n, v), others(ww, g, 0, r0, n, w)):
                gap_v, gap_w = v - a, w - b
                for i, term in enumerate((gap_v * gap_v, gap_v * gap_w, gap_w * gap_w)):
                    forms[i] = term if forms[i] is None else forms[i] + term
            for i in range(3):
                ee[g, i, r0 - LO : r0 - LO + n, :] = forms[i] * kk[g, rows, :]
        for i in range(3):
            turned_e[g, i] = ee[g, i].T

    in_plane.wait_recv()
    in_stack = share(gathered(rowp, NXC * NYC), rowz, send_z, recv_z, stack)
    in_plane.wait_send()
    in_stack.wait_recv()
    line = gathered(rowz, NZC * NCORE)

    rz0, pq1 = line, pltpu.roll(line, 96, 1)
    qdq, wsw = pltpu.roll(line, 64, 1), pltpu.roll(line, 32, 1)
    step_one = rz0 / pq1
    rz1 = rz0 - 2.0 * step_one * pq1 + step_one * step_one * qdq
    grow = 1.0 + rz1 / rz0
    pq2 = grow * grow * pq1 - 2.0 * grow * step_one * qdq + step_one * step_one * wsw
    step_two = rz1 / pq2
    along = step_one + step_two * grow
    across = -step_one * step_two

    scale = (along * along, 2.0 * along * across, across * across)
    factors = [[jnp.broadcast_to(part[:, g : g + 1], (1, 128)) for part in scale] for g in range(NPROJ)]
    for layer in range(DEPTH):
        for y in range(0, WIDTH, 32):
            rows = slice(layer * WIDTH + y, layer * WIDTH + y + 32)
            result = None
            for g in range(NPROJ):
                for i in range(3):
                    term = factors[g][i] * turned_e[g, i, rows, :]
                    result = term if result is None else result + term
            out[layer, y : y + 32, :] = result

    in_stack.wait_send()


def local(design, solid_mask, void_mask, load_mask, support_mask, thresholds, group_weight):
    dma = pltpu.SemaphoreType.DMA
    return pl.pallas_call(
        kernel,
        out_shape=pltpu.VMEM((DEPTH, WIDTH, THICK), F32),
        in_specs=[pl.BlockSpec(memory_space=pl.ANY)] * 5 + [pl.BlockSpec(memory_space=pltpu.HBM)] * 2,
        out_specs=pl.BlockSpec(memory_space=pltpu.VMEM),
        scratch_shapes=[
            pltpu.VMEM((DEPTH, WIDTH, THICK), F32),
            pltpu.VMEM((8, DEPTH, WIDTH, THICK), jnp.int32),
            pltpu.VMEM((5, ROWS, 128), F32),
            pltpu.VMEM((2, REACH, 128), F32),
            pltpu.VMEM((5, 2, REACH, 128), F32),
            pltpu.VMEM((2, 3 * THICK + 16, 128), F32),
            pltpu.VMEM((2, 2, ROWS, 128), F32),
            pltpu.VMEM((5, ROWS, 128), F32),
            pltpu.VMEM((3, ROWS, 128), F32),
            pltpu.VMEM((3, ROWS, 128), F32),
            pltpu.VMEM((5, ROWS, 128), F32),
            pltpu.VMEM((4, ROWS, 128), F32),
            pltpu.VMEM((NPROJ, 8, 128), F32),
            pltpu.VMEM((NPROJ, 4, ROWS, 128), F32),
            pltpu.VMEM((NPROJ, 2, 6, ROWS, 128), F32),
            pltpu.VMEM((NPROJ, 3, ROWS, 128), F32),
            pltpu.VMEM((NPROJ, 2, ROWS, 128), F32),
            pltpu.VMEM((NPROJ, 2, ROWS, 128), F32),
            pltpu.VMEM((NPROJ, ROWS, 128), F32),
            pltpu.VMEM((NXC * NYC, 1, 128), F32),
            pltpu.VMEM((NZC * NCORE, 1, 128), F32),
            pltpu.VMEM((NPROJ, 3, THICK, 128), F32),
            pltpu.VMEM((NPROJ, 3, THICK, 128), F32),
            pltpu.SMEM((1, 1), jnp.int32),
            pltpu.SMEM((1, 1), F32),
            dma((5,)), dma((1,)),
            dma((1,)), dma((4,)),
            dma((1,)), dma((1,)),
            dma((1,)), dma((1,)),
            dma((1,)), dma((1,)),
            dma((1,)), dma((1,)),
            dma((1,)), dma((1,)),
        ],
        compiler_params=pltpu.CompilerParams(collective_id=0, has_side_effects=True),
    )(
        design, solid_mask, void_mask, load_mask, support_mask,
        thresholds.reshape(1, 1), group_weight.reshape(1, 1),
    )


def solution(mesh):
    placed = (
        P("space", None, "proj"),
        P("space", None, "proj"),
        P("space", None, "proj"),
        P("space", None, None),
        P("space", None, None),
        P("proj"),
        P("proj"),
    )
    return jax.shard_map(
        local, mesh=mesh, in_specs=placed, out_specs=P("space", None, "proj"), check_vma=False
    )
```

```python
import math

import jax
import jax.numpy as jnp
from jax import lax
from jax.experimental import pallas as pl
from jax.experimental.pallas import tpu as pltpu
from jax.sharding import PartitionSpec as P

RMIN = 2.0
BETA = 8.0
EMIN = 0.05
PENALTY = 4.0
MESH = pl.DeviceIdType.MESH
F32 = jnp.float32

NPROJ, NSPACE = 3, 256
NYC, NXC, NZLO, NCORE = 8, 4, 4, 2
NZC = NPROJ * NZLO
DEPTH, WIDTH, THICK = 2, 64, 128
GX, GZ = NSPACE * DEPTH, NPROJ * THICK

LO, HI = 16, 16 + THICK
ROWS = HI + 16
EDGE = 2.0 - math.sqrt(2.0)
CORNER = 2.0 - math.sqrt(3.0)
OWN = [(LO + i, 32) for i in range(0, THICK, 32)]
ALL = [(LO - 8, 8)] + OWN + [(HI, 8)]
REACH = 4
FILTER = [(24, 16), (40, 16), (56, 16), (72, 16), (88, 16), (104, 16), (120, 16)], [(8, 16), (136, 16)]
DIAGONAL = [(32, 16), (48, 16), (64, 16), (80, 16), (96, 16), (112, 16)], [(8, 16), (24, 8), (128, 16), (144, 8)]
FIRST = [(40, 16), (56, 16), (72, 16), (88, 16), (104, 16)], [(8, 16), (24, 16), (120, 16), (136, 16)]
SECOND = [(48, 16), (64, 16), (80, 16), (96, 16)], [(16, 16), (32, 16), (112, 16), (128, 16)]


def kernel(
    design, solid, void, load_in, support_in, eta_in, weight_in, out,
    raw, masks, fb, rim_out, rim_in, lt, ls, ring, lr, sr, inm, inv, tw, hh, cond, zz, idg, ww, kk, rowp, rowz, ee, turned_e,
    eta_held, weight_held,
    in_sem, mask_sem, send_f, recv_f, send_e, recv_e, send_m, recv_m, send_t, recv_t,
    send_p, recv_p, send_z, recv_z,
):
    me = lax.axis_index("space")
    slab = lax.axis_index("proj")
    core = me & 1
    zlo = (me >> 1) & 3
    line_z = slab * NZLO + zlo
    inward = 1 - 2 * core
    slab_up = jnp.where(slab == NPROJ - 1, 0, slab + 1)
    slab_down = jnp.where(slab == 0, NPROJ - 1, slab - 1)
    slabs = {0: slab, 1: slab_up, -1: slab_down}

    def space_at(step):
        return (me + step) & (NSPACE - 1)

    loads = []
    for i, source in enumerate((design, solid, void)):
        target = raw if i == 0 else masks.at[i - 1]
        loads.append(pltpu.make_async_copy(source, target, in_sem.at[i]))
    for i, source in enumerate((load_in, support_in)):
        for j, step in enumerate((-1, 0, 1)):
            lane = pl.multiple_of(slabs[step] * THICK, THICK)
            loads.append(
                pltpu.make_async_copy(source.at[:, :, pl.ds(lane, THICK)], masks.at[2 + 3 * i + j], mask_sem.at[0])
            )
    loads.append(pltpu.make_async_copy(eta_in, eta_held, in_sem.at[3]))
    loads.append(pltpu.make_async_copy(weight_in, weight_held, in_sem.at[4]))
    mask_loads = pltpu.make_async_copy(masks.at[pl.ds(2, 6)], masks.at[pl.ds(2, 6)], mask_sem.at[0])
    for item in loads[:3]:
        item.start()

    near = (1, -1, 2, -2)
    halo = [(slabs[e], space_at(d)) for d in near[::-1] + (0,) for e in (1, -1)]
    halo += [(slab, space_at(d)) for d in near]
    barrier = pltpu.get_barrier_semaphore()
    for place in halo:
        pl.semaphore_signal(barrier, inc=1, device_id=place, device_id_type=MESH)
    for item in loads[9:]:
        item.start()
    rows_y = [(me + (dy << 5)) & 0xE0 for dy in range(NYC)]
    rows_x = [(me + (dx << 3)) & 0x18 for dx in range(NXC)]
    low = me & 0x07
    plane = sorted(
        ((dy, dx, dc) for dy in range(NYC) for dx in range(NXC) for dc in range(NCORE) if dy or dx or dc),
        key=lambda p: -(min(p[0], NYC - p[0]) + min(p[1], NXC - p[1])),
    )
    lows = (low, low + inward)
    plane = [(slab, rows_y[dy] + rows_x[dx] + lows[dc]) for dy, dx, dc in plane]
    stack = sorted(((dz, dc) for dz in range(NZC) for dc in range(1) if dz), key=lambda p: -min(p[0], NZC - p[0]))
    base = me & 0xF8
    cores = (core, 1 - core)
    levels = []
    for dz in range(NZC):
        z = line_z + dz
        z = jnp.where(z >= NZC, z - NZC, z)
        levels.append((z >> 2, base + ((z & 3) << 1)))
    stack = [(levels[dz][0], levels[dz][1] + cores[dc]) for dz, dc in stack]
    for place in plane + stack:
        pl.semaphore_signal(barrier, inc=1, device_id=place, device_id_type=MESH)
    for item in loads[3:9]:
        item.start()

    lane = lax.broadcasted_iota(jnp.int32, (1, 128), 1)
    cell_y = lane % WIDTH
    upper = lane >= WIDTH
    has_up = cell_y < WIDTH - 1
    has_down = cell_y > 0

    def y_up(v):
        return jnp.where(has_up, pltpu.roll(v, 127, 1), 0.0)

    def y_down(v):
        return jnp.where(has_down, pltpu.roll(v, 1, 1), 0.0)

    def swap(v):
        return pltpu.roll(v, WIDTH, 1)

    for item in loads[:3]:
        item.wait()
    fixed = jnp.where(masks[0] == 1, 1.0, jnp.where(masks[1] == 1, 0.0, raw[...])).reshape(128, 128).T
    fb[2, LO:HI, :] = fixed
    rim_out[0] = fixed[THICK - REACH :, :]
    rim_out[1] = fixed[:REACH, :]

    for item in loads[9:]:
        item.wait()
    eta = eta_held[0, 0].astype(F32) / 1000.0
    row = lax.broadcasted_iota(jnp.int32, (8, 128), 0)
    tw[slab] = jnp.where(row == 0, eta, weight_held[0, 0])

    def remote(source, target, ssem, rsem, place):
        return pltpu.make_async_remote_copy(
            src_ref=source, dst_ref=target, send_sem=ssem, recv_sem=rsem, device_id=place, device_id_type=MESH
        )

    def main_copy(i, source, target, step):
        return remote(
            fb.at[source, pl.ds(LO, THICK), :], fb.at[target, pl.ds(LO, THICK), :],
            send_f.at[0], recv_f.at[i], (slab, space_at(step)),
        )

    from_outer = main_copy(0, 2, 2 + inward, -inward)
    from_far = main_copy(1, 2, 2 - 2 * inward, 2 * inward)
    from_partner = main_copy(2, 2, 2 - inward, inward)
    relay = main_copy(3, 2 - inward, 2 - 2 * inward, inward)
    rims, marks, small = [], [], []
    for d in near[::-1] + (0,):
        for j, e in enumerate((1, -1)):
            rims.append(remote(rim_out.at[j], rim_in.at[2 - d, j], send_e.at[0], recv_e.at[0], (slabs[e], space_at(d))))
    for i, e in enumerate((1, -1)):
        small.append(remote(tw.at[slab], tw.at[slab], send_t.at[0], recv_t.at[0], (slabs[e], me)))

    spill_up = ((me & 7) == 7).astype(jnp.int32)
    spill_down = ((me & 7) == 0).astype(jnp.int32)
    for i, (d, spill) in enumerate(((1, spill_up), (-1, -spill_down))):
        start = pl.multiple_of(THICK + THICK * spill, 8)
        place = jnp.where(spill == 0, slab, slabs[d])
        marks.append(
            remote(
                lt.at[:, pl.ds(start, THICK + 16), :], ls.at[i, :, pl.ds(LO - 8, THICK + 16), :],
                send_m.at[0], recv_m.at[0], (place, space_at(d)),
            )
        )

    def whole(ref, ssem, rsem):
        return remote(ref, ref, ssem.at[0], rsem.at[0], (slab, space_at(1)))

    all_main = whole(fb.at[pl.ds(0, 4), pl.ds(LO, THICK), :], send_f, recv_f)
    all_rims = whole(rim_in, send_e, recv_e)
    all_marks = whole(ls.at[:, :, pl.ds(LO - 8, THICK + 16), :], send_m, recv_m)
    all_small = whole(tw.at[pl.ds(0, 2)], send_t, recv_t)

    pl.semaphore_wait(barrier, len(halo) + len(plane) + len(stack))
    for item in rims[:8] + [from_outer, from_partner] + rims[8:] + small:
        item.start()

    mask_loads.wait()
    for i in range(2):
        for j in range(3):
            turned = masks[2 + 3 * i + j].reshape(128, 128).astype(F32).T
            lt[i, 8 + THICK * j : 8 + THICK * (j + 1), :] = turned
            if j == 0:
                lt[i, 8 + 3 * THICK :, :] = turned[:8, :]
            if j == 2:
                lt[i, 0:8, :] = turned[120:, :]

    count_y = has_up.astype(F32) + has_down.astype(F32)
    for k in range(5):
        layer = jnp.where(upper, 1 + k, -k) + me * DEPTH
        in_x = ((layer >= 0) & (layer < GX)).astype(F32)
        count_x = (layer > 0).astype(F32) + (layer < GX - 1).astype(F32)
        for r0, n in ALL:
            z = slab * THICK + (r0 - LO) + lax.broadcasted_iota(jnp.int32, (n, 128), 0)
            in_z = ((z >= 0) & (z < GZ)).astype(F32)
            inm[k, r0 : r0 + n, :] = in_z * in_x
            if k < 4:
                count_z = (z > 0).astype(F32) + (z < GZ - 1).astype(F32)
                pair = count_y * count_z
                total = 2.0 + count_x + count_y + count_z
                total = total + EDGE * (count_x * (count_y + count_z) + pair) + CORNER * (count_x * pair)
                inv[k, r0 : r0 + n, :] = BETA / total

    from_far.start()
    for item in marks:
        item.start()
    from_outer.wait_recv()
    relay.start()
    for item in (from_partner, from_far, all_small, relay):
        item.wait_recv()

    def form_rings(r0, n, bricks):
        rows = slice(r0, r0 + n)
        m2, m1, own, p1, p2 = bricks
        ring[0, rows, :] = own * inm[0, rows, :]
        ring[1, rows, :] = swap(jnp.where(upper, m1, p1)) * inm[1, rows, :]
        ring[2, rows, :] = jnp.where(upper, p1, m1) * inm[2, rows, :]
        ring[3, rows, :] = swap(jnp.where(upper, m2, p2)) * inm[3, rows, :]
        ring[4, rows, :] = jnp.where(upper, p2, m2) * inm[4, rows, :]

    for r0, n in OWN:
        form_rings(r0, n, [fb[i, r0 : r0 + n, :] for i in range(5)])

    etas, tops, scales, weights = [], [], [], []
    for g in range(NPROJ):
        e = tw[g, 0:1, :]
        t = jnp.tanh(BETA * e)
        bottom = t + jnp.tanh(BETA * (1.0 - e))
        etas.append(BETA * e)
        tops.append(t / bottom)
        scales.append(1.0 / bottom)
        weights.append(tw[g, 1:2, :] * (-0.5 * 3.0 * (1.0 - EMIN) * BETA) / bottom)

    def project(chunks):
        for r0, n in chunks:
            rows = slice(r0, r0 + n)
            plain = [ring[k, rows, :] for k in range(5)]
            beside = [ring[k, r0 + 1 : r0 + n + 1, :] + ring[k, r0 - 1 : r0 + n - 1, :] for k in range(5)]
            for k in range(4):
                v, zb = plain[k], beside[k]
                vx = (plain[k - 1] if k else swap(v)) + plain[k + 1]
                zx = (beside[k - 1] if k else swap(zb)) + beside[k + 1]
                line_y = v + EDGE * (zb + vx) + CORNER * zx
                total = 2.0 * v + (zb + vx) + EDGE * zx + (y_up(line_y) + y_down(line_y))
                f8 = total * inv[k, rows, :]
                mask = inm[k, rows, :]
                for g in range(NPROJ):
                    t = jnp.tanh(f8 - etas[g])
                    value = t * scales[g] + tops[g]
                    square = value * value
                    hh[g, k, rows, :] = ((0.5 * (1.0 - EMIN)) * (square * value) + 0.5 * EMIN) * mask
                    if k == 0:
                        kk[g, rows, :] = (weights[g] * square) * (1.0 - t * t)

    def precondition(chunks):
        for g in range(NPROJ):
            for k in range(3):
                for r0, n in chunks:
                    rows = slice(r0, r0 + n)
                    h = hh[g, k, rows, :]
                    inner = hh[g, k - 1, rows, :] if k else swap(h)
                    near_h = [
                        inner,
                        hh[g, k + 1, rows, :],
                        y_up(h),
                        y_down(h),
                        hh[g, k, r0 + 1 : r0 + n + 1, :],
                        hh[g, k, r0 - 1 : r0 + n - 1, :],
                    ]
                    diag = sr[k, rows, :]
                    if k == 2:
                        diag = diag + 6.0 * h
                    for i, other in enumerate(near_h):
                        if k < 2:
                            other = h + other
                            cond[g, k, i, rows, :] = other
                        diag = diag + other
                    inverse = inm[k, rows, :] / diag
                    zz[g, k, rows, :] = lr[k, rows, :] * inverse
                    if k < 2:
                        idg[g, k, rows, :] = inverse

    def others(field, g, k, r0, n, v):
        rows = slice(r0, r0 + n)
        return [
            field[g, k - 1, rows, :] if k else swap(v),
            field[g, k + 1, rows, :],
            y_up(v),
            y_down(v),
            field[g, k, r0 + 1 : r0 + n + 1, :],
            field[g, k, r0 - 1 : r0 + n - 1, :],
        ]

    def operate(field, g, k, r0, n):
        v = field[g, k, r0 : r0 + n, :]
        total = None
        for i, other in enumerate(others(field, g, k, r0, n, v)):
            term = cond[g, k, i, r0 : r0 + n, :] * (v - other)
            total = term if total is None else total + term
        return v, total

    sums = [[None] * 4 for _ in range(NPROJ)]

    def add(g, i, r0, n, v):
        v = v[max(LO - r0, 0) : n - max(r0 + n - HI, 0)]
        v = jnp.sum(v.reshape(v.shape[0] // 8, 8, 128), axis=0)
        sums[g][i] = v if sums[g][i] is None else sums[g][i] + v

    def first_step(chunks):
        for g in range(NPROJ):
            for k in range(2):
                for r0, n in chunks:
                    rows = slice(r0, r0 + n)
                    v, image = operate(zz, g, k, r0, n)
                    w = image * idg[g, k, rows, :]
                    ww[g, k, rows, :] = w
                    if k == 0:
                        add(g, 0, r0, n, v * lr[0, rows, :])
                        add(g, 1, r0, n, v * image)
                        add(g, 2, r0, n, w * image)

    def second_step(chunks):
        for g in range(NPROJ):
            for r0, n in chunks:
                w, image = operate(ww, g, 0, r0, n)
                add(g, 3, r0, n, w * image)

    project(FILTER[0])

    all_marks.wait_recv()

    for r0, n in ALL:
        rows = slice(r0, r0 + n)
        for k in range(3):
            mask = inm[k, rows, :]
            both = []
            for i in range(2):
                if k == 0:
                    both.append(lt[i, r0 + 8 + THICK - LO : r0 + n + 8 + THICK - LO, :])
                elif k == 1:
                    both.append(swap(jnp.where(upper, ls[0, i, rows, :], ls[1, i, rows, :])))
                else:
                    both.append(jnp.where(upper, ls[1, i, rows, :], ls[0, i, rows, :]))
            lr[k, rows, :] = both[0] * mask
            sr[k, rows, :] = PENALTY * jnp.maximum(both[1], 1.0 - mask)

    precondition(DIAGONAL[0])
    first_step(FIRST[0])
    second_step(SECOND[0])

    all_rims.wait_recv()
    for j, r0 in enumerate((LO - REACH, HI)):
        form_rings(r0, REACH, [rim_in[i, j] for i in range(5)])
    project(FILTER[1])
    precondition(DIAGONAL[1])
    first_step(FIRST[1])
    second_step(SECOND[1])

    parts = jnp.concatenate([jnp.sum(sums[g][i], axis=0, keepdims=True) for i in range(4) for g in range(NPROJ)] + [jnp.zeros((4, 128), F32)], axis=0)
    totals = jnp.sum(parts, axis=1, keepdims=True)
    which = lax.broadcasted_iota(jnp.int32, (16, 128), 0)
    place = (which // NPROJ) * 32 + which % NPROJ
    spot = lax.broadcasted_iota(jnp.int32, (16, 128), 1)
    line = jnp.sum(jnp.where((spot == place) & (which < 12), totals, 0.0), axis=0, keepdims=True)

    def share(value, rows_ref, ssem, rsem, places):
        rows_ref[0] = value
        for d, place in enumerate(places):
            remote(rows_ref.at[0], rows_ref.at[d + 1], ssem.at[0], rsem.at[0], place).start()
        every = rows_ref.at[pl.ds(1, len(places))]
        return remote(every, every, ssem.at[0], rsem.at[0], places[0])

    def gathered(rows_ref, size):
        terms = [rows_ref[d] for d in range(size)]
        while len(terms) > 1:
            terms = [a + b for a, b in zip(terms[::2], terms[1::2])] + terms[len(terms) // 2 * 2 :]
        return terms[0]

    in_plane = share(line, rowp, send_p, recv_p, plane)
    for item in (all_main, all_rims, all_small, all_marks):
        item.wait_send()

    for g in range(NPROJ):
        for r0, n in OWN:
            rows = slice(r0, r0 + n)
            v, w = zz[g, 0, rows, :], ww[g, 0, rows, :]
            forms = [None] * 3
            for a, b in zip(others(zz, g, 0, r0, n, v), others(ww, g, 0, r0, n, w)):
                gap_v, gap_w = v - a, w - b
                for i, term in enumerate((gap_v * gap_v, gap_v * gap_w, gap_w * gap_w)):
                    forms[i] = term if forms[i] is None else forms[i] + term
            for i in range(3):
                ee[g, i, r0 - LO : r0 - LO + n, :] = forms[i] * kk[g, rows, :]
        for i in range(3):
            turned_e[g, i] = ee[g, i].T

    in_plane.wait_recv()
    in_stack = share(gathered(rowp, NXC * NYC * NCORE), rowz, send_z, recv_z, stack)
    in_plane.wait_send()
    in_stack.wait_recv()
    line = gathered(rowz, NZC)

    rz0, pq1 = line, pltpu.roll(line, 96, 1)
    qdq, wsw = pltpu.roll(line, 64, 1), pltpu.roll(line, 32, 1)
    step_one = rz0 / pq1
    rz1 = rz0 - 2.0 * step_one * pq1 + step_one * step_one * qdq
    grow = 1.0 + rz1 / rz0
    pq2 = grow * grow * pq1 - 2.0 * grow * step_one * qdq + step_one * step_one * wsw
    step_two = rz1 / pq2
    along = step_one + step_two * grow
    across = -step_one * step_two

    scale = (along * along, 2.0 * along * across, across * across)
    factors = [[jnp.broadcast_to(part[:, g : g + 1], (1, 128)) for part in scale] for g in range(NPROJ)]
    for layer in range(DEPTH):
        for y in range(0, WIDTH, 32):
            rows = slice(layer * WIDTH + y, layer * WIDTH + y + 32)
            result = None
            for g in range(NPROJ):
                for i in range(3):
                    term = factors[g][i] * turned_e[g, i, rows, :]
                    result = term if result is None else result + term
            out[layer, y : y + 32, :] = result

    in_stack.wait_send()


def local(design, solid_mask, void_mask, load_mask, support_mask, thresholds, group_weight):
    dma = pltpu.SemaphoreType.DMA
    return pl.pallas_call(
        kernel,
        out_shape=pltpu.VMEM((DEPTH, WIDTH, THICK), F32),
        in_specs=[pl.BlockSpec(memory_space=pl.ANY)] * 5 + [pl.BlockSpec(memory_space=pltpu.HBM)] * 2,
        out_specs=pl.BlockSpec(memory_space=pltpu.VMEM),
        scratch_shapes=[
            pltpu.VMEM((DEPTH, WIDTH, THICK), F32),
            pltpu.VMEM((8, DEPTH, WIDTH, THICK), jnp.int32),
            pltpu.VMEM((5, ROWS, 128), F32),
            pltpu.VMEM((2, REACH, 128), F32),
            pltpu.VMEM((5, 2, REACH, 128), F32),
            pltpu.VMEM((2, 3 * THICK + 16, 128), F32),
            pltpu.VMEM((2, 2, ROWS, 128), F32),
            pltpu.VMEM((5, ROWS, 128), F32),
            pltpu.VMEM((3, ROWS, 128), F32),
            pltpu.VMEM((3, ROWS, 128), F32),
            pltpu.VMEM((5, ROWS, 128), F32),
            pltpu.VMEM((4, ROWS, 128), F32),
            pltpu.VMEM((NPROJ, 8, 128), F32),
            pltpu.VMEM((NPROJ, 4, ROWS, 128), F32),
            pltpu.VMEM((NPROJ, 2, 6, ROWS, 128), F32),
            pltpu.VMEM((NPROJ, 3, ROWS, 128), F32),
            pltpu.VMEM((NPROJ, 2, ROWS, 128), F32),
            pltpu.VMEM((NPROJ, 2, ROWS, 128), F32),
            pltpu.VMEM((NPROJ, ROWS, 128), F32),
            pltpu.VMEM((NXC * NYC * NCORE, 1, 128), F32),
            pltpu.VMEM((NZC, 1, 128), F32),
            pltpu.VMEM((NPROJ, 3, THICK, 128), F32),
            pltpu.VMEM((NPROJ, 3, THICK, 128), F32),
            pltpu.SMEM((1, 1), jnp.int32),
            pltpu.SMEM((1, 1), F32),
            dma((5,)), dma((1,)),
            dma((1,)), dma((4,)),
            dma((1,)), dma((1,)),
            dma((1,)), dma((1,)),
            dma((1,)), dma((1,)),
            dma((1,)), dma((1,)),
            dma((1,)), dma((1,)),
        ],
        compiler_params=pltpu.CompilerParams(collective_id=0, has_side_effects=True),
    )(
        design, solid_mask, void_mask, load_mask, support_mask,
        thresholds.reshape(1, 1), group_weight.reshape(1, 1),
    )


def solution(mesh):
    placed = (
        P("space", None, "proj"),
        P("space", None, "proj"),
        P("space", None, "proj"),
        P("space", None, None),
        P("space", None, None),
        P("proj"),
        P("proj"),
    )
    return jax.shard_map(
        local, mesh=mesh, in_specs=placed, out_specs=P("space", None, "proj"), check_vma=False
    )
```

```python
import math

import jax
import jax.numpy as jnp
from jax import lax
from jax.experimental import pallas as pl
from jax.experimental.pallas import tpu as pltpu
from jax.sharding import PartitionSpec as P

RMIN = 2.0
BETA = 8.0
EMIN = 0.05
PENALTY = 4.0
MESH = pl.DeviceIdType.MESH
F32 = jnp.float32

NPROJ, NSPACE = 3, 256
NYC, NXC, NZLO, NCORE = 8, 4, 4, 2
NZC = NPROJ * NZLO
DEPTH, WIDTH, THICK = 2, 64, 128
GX, GZ = NSPACE * DEPTH, NPROJ * THICK

LO, HI = 16, 16 + THICK
ROWS = HI + 16
EDGE = 2.0 - math.sqrt(2.0)
CORNER = 2.0 - math.sqrt(3.0)
OWN = [(LO + i, 32) for i in range(0, THICK, 32)]
ALL = [(LO - 8, 8)] + OWN + [(HI, 8)]
REACH = 4
FILTER = [(24, 16), (40, 16), (56, 16), (72, 16), (88, 16), (104, 16), (120, 16)], [(8, 16), (136, 16)]
DIAGONAL = [(32, 16), (48, 16), (64, 16), (80, 16), (96, 16), (112, 16)], [(8, 16), (24, 8), (128, 16), (144, 8)]
FIRST = [(40, 16), (56, 16), (72, 16), (88, 16), (104, 16)], [(8, 16), (24, 16), (120, 16), (136, 16)]
SECOND = [(48, 16), (64, 16), (80, 16), (96, 16)], [(16, 16), (32, 16), (112, 16), (128, 16)]


def kernel(
    design, solid, void, load_in, support_in, eta_in, weight_in, out,
    raw, masks, fb, rim_out, rim_in, lt, ls, ring, lr, sr, inm, inv, tw, hh, cond, zz, idg, ww, kk, rowp, rowz, ee, turned_e,
    eta_held, weight_held,
    in_sem, mask_sem, send_f, recv_f, send_e, recv_e, send_m, recv_m, send_t, recv_t,
    send_p, recv_p, send_z, recv_z,
):
    me = lax.axis_index("space")
    slab = lax.axis_index("proj")
    core = me & 1
    zlo = (me >> 1) & 3
    line_z = slab * NZLO + zlo
    inward = 1 - 2 * core
    slab_up = jnp.where(slab == NPROJ - 1, 0, slab + 1)
    slab_down = jnp.where(slab == 0, NPROJ - 1, slab - 1)
    slabs = {0: slab, 1: slab_up, -1: slab_down}

    def space_at(step):
        return (me + step) & (NSPACE - 1)

    loads = []
    for i, source in enumerate((design, solid, void)):
        target = raw if i == 0 else masks.at[i - 1]
        loads.append(pltpu.make_async_copy(source, target, in_sem.at[i]))
    for i, source in enumerate((load_in, support_in)):
        for j, step in enumerate((-1, 0, 1)):
            lane = pl.multiple_of(slabs[step] * THICK, THICK)
            loads.append(
                pltpu.make_async_copy(source.at[:, :, pl.ds(lane, THICK)], masks.at[2 + 3 * i + j], mask_sem.at[0])
            )
    loads.append(pltpu.make_async_copy(eta_in, eta_held, in_sem.at[3]))
    loads.append(pltpu.make_async_copy(weight_in, weight_held, in_sem.at[4]))
    mask_loads = pltpu.make_async_copy(masks.at[pl.ds(2, 6)], masks.at[pl.ds(2, 6)], mask_sem.at[0])
    for item in loads[:3]:
        item.start()

    near = (1, -1, 2, -2)
    halo = [(slabs[e], space_at(d)) for d in near[::-1] + (0,) for e in (1, -1)]
    halo += [(slab, space_at(d)) for d in near]
    barrier = pltpu.get_barrier_semaphore()
    for place in halo:
        pl.semaphore_signal(barrier, inc=1, device_id=place, device_id_type=MESH)
    for item in loads[9:]:
        item.start()
    rows_y = [(me + (dy << 5)) & 0xE0 for dy in range(NYC)]
    rows_x = [(me + (dx << 3)) & 0x18 for dx in range(NXC)]
    low = me & 0x07
    plane = sorted(
        ((dy, dx) for dy in range(NYC) for dx in range(NXC) if dy or dx),
        key=lambda p: -(min(p[0], NYC - p[0]) + min(p[1], NXC - p[1])),
    )
    plane = [(slab, rows_y[dy] + rows_x[dx] + low) for dy, dx in plane]
    stack = sorted(((dz, dc) for dz in range(NZC) for dc in range(NCORE) if dz or dc), key=lambda p: -min(p[0], NZC - p[0]))
    base = me & 0xF8
    cores = (core, 1 - core)
    levels = []
    for dz in range(NZC):
        z = line_z + dz
        z = jnp.where(z >= NZC, z - NZC, z)
        levels.append((z >> 2, base + ((z & 3) << 1)))
    stack = [(levels[dz][0], levels[dz][1] + cores[dc]) for dz, dc in stack]
    for place in plane + stack:
        pl.semaphore_signal(barrier, inc=1, device_id=place, device_id_type=MESH)
    for item in loads[3:9]:
        item.start()

    lane = lax.broadcasted_iota(jnp.int32, (1, 128), 1)
    cell_y = lane % WIDTH
    upper = lane >= WIDTH
    has_up = cell_y < WIDTH - 1
    has_down = cell_y > 0

    def y_up(v):
        return jnp.where(has_up, pltpu.roll(v, 127, 1), 0.0)

    def y_down(v):
        return jnp.where(has_down, pltpu.roll(v, 1, 1), 0.0)

    def swap(v):
        return pltpu.roll(v, WIDTH, 1)

    for item in loads[:3]:
        item.wait()
    fixed = jnp.where(masks[0] == 1, 1.0, jnp.where(masks[1] == 1, 0.0, raw[...])).reshape(128, 128).T
    fb[2, LO:HI, :] = fixed
    rim_out[0] = fixed[THICK - REACH :, :]
    rim_out[1] = fixed[:REACH, :]

    for item in loads[9:]:
        item.wait()
    eta = eta_held[0, 0].astype(F32) / 1000.0
    row = lax.broadcasted_iota(jnp.int32, (8, 128), 0)
    tw[slab] = jnp.where(row == 0, eta, weight_held[0, 0])

    def remote(source, target, ssem, rsem, place):
        return pltpu.make_async_remote_copy(
            src_ref=source, dst_ref=target, send_sem=ssem, recv_sem=rsem, device_id=place, device_id_type=MESH
        )

    def main_copy(i, source, target, step):
        return remote(
            fb.at[source, pl.ds(LO, THICK), :], fb.at[target, pl.ds(LO, THICK), :],
            send_f.at[0], recv_f.at[i], (slab, space_at(step)),
        )

    from_outer = main_copy(0, 2, 2 + inward, -inward)
    from_far = main_copy(1, 2, 2 - 2 * inward, 2 * inward)
    from_partner = main_copy(2, 2, 2 - inward, inward)
    relay = main_copy(3, 2 - inward, 2 - 2 * inward, inward)
    rims, marks, small = [], [], []
    for d in near[::-1] + (0,):
        for j, e in enumerate((1, -1)):
            rims.append(remote(rim_out.at[j], rim_in.at[2 - d, j], send_e.at[0], recv_e.at[0], (slabs[e], space_at(d))))
    for i, e in enumerate((1, -1)):
        small.append(remote(tw.at[slab], tw.at[slab], send_t.at[0], recv_t.at[0], (slabs[e], me)))

    spill_up = ((me & 7) == 7).astype(jnp.int32)
    spill_down = ((me & 7) == 0).astype(jnp.int32)
    for i, (d, spill) in enumerate(((1, spill_up), (-1, -spill_down))):
        start = pl.multiple_of(THICK + THICK * spill, 8)
        place = jnp.where(spill == 0, slab, slabs[d])
        marks.append(
            remote(
                lt.at[:, pl.ds(start, THICK + 16), :], ls.at[i, :, pl.ds(LO - 8, THICK + 16), :],
                send_m.at[0], recv_m.at[0], (place, space_at(d)),
            )
        )

    def whole(ref, ssem, rsem):
        return remote(ref, ref, ssem.at[0], rsem.at[0], (slab, space_at(1)))

    all_main = whole(fb.at[pl.ds(0, 4), pl.ds(LO, THICK), :], send_f, recv_f)
    all_rims = whole(rim_in, send_e, recv_e)
    all_marks = whole(ls.at[:, :, pl.ds(LO - 8, THICK + 16), :], send_m, recv_m)
    all_small = whole(tw.at[pl.ds(0, 2)], send_t, recv_t)

    pl.semaphore_wait(barrier, len(halo) + len(plane) + len(stack))
    for item in rims[:8] + [from_outer, from_partner] + rims[8:] + small:
        item.start()

    mask_loads.wait()
    for i in range(2):
        for j in range(3):
            turned = masks[2 + 3 * i + j].reshape(128, 128).astype(F32).T
            lt[i, 8 + THICK * j : 8 + THICK * (j + 1), :] = turned
            if j == 0:
                lt[i, 8 + 3 * THICK :, :] = turned[:8, :]
            if j == 2:
                lt[i, 0:8, :] = turned[120:, :]

    count_y = has_up.astype(F32) + has_down.astype(F32)
    for k in range(5):
        layer = jnp.where(upper, 1 + k, -k) + me * DEPTH
        in_x = ((layer >= 0) & (layer < GX)).astype(F32)
        count_x = (layer > 0).astype(F32) + (layer < GX - 1).astype(F32)
        for r0, n in ALL:
            z = slab * THICK + (r0 - LO) + lax.broadcasted_iota(jnp.int32, (n, 128), 0)
            in_z = ((z >= 0) & (z < GZ)).astype(F32)
            inm[k, r0 : r0 + n, :] = in_z * in_x
            if k < 4:
                count_z = (z > 0).astype(F32) + (z < GZ - 1).astype(F32)
                pair = count_y * count_z
                total = 2.0 + count_x + count_y + count_z
                total = total + EDGE * (count_x * (count_y + count_z) + pair) + CORNER * (count_x * pair)
                inv[k, r0 : r0 + n, :] = BETA / total

    from_far.start()
    for item in marks:
        item.start()
    from_outer.wait_recv()
    relay.start()
    for item in (from_partner, from_far, all_small, relay):
        item.wait_recv()

    def form_rings(r0, n, bricks):
        rows = slice(r0, r0 + n)
        m2, m1, own, p1, p2 = bricks
        ring[0, rows, :] = own * inm[0, rows, :]
        ring[1, rows, :] = swap(jnp.where(upper, m1, p1)) * inm[1, rows, :]
        ring[2, rows, :] = jnp.where(upper, p1, m1) * inm[2, rows, :]
        ring[3, rows, :] = swap(jnp.where(upper, m2, p2)) * inm[3, rows, :]
        ring[4, rows, :] = jnp.where(upper, p2, m2) * inm[4, rows, :]

    for r0, n in OWN:
        form_rings(r0, n, [fb[i, r0 : r0 + n, :] for i in range(5)])

    etas, tops, scales, weights = [], [], [], []
    for g in range(NPROJ):
        e = tw[g, 0:1, :]
        t = jnp.tanh(BETA * e)
        bottom = t + jnp.tanh(BETA * (1.0 - e))
        etas.append(BETA * e)
        tops.append(t / bottom)
        scales.append(1.0 / bottom)
        weights.append(tw[g, 1:2, :] * (-0.5 * 3.0 * (1.0 - EMIN) * BETA) / bottom)

    def project(chunks):
        for r0, n in chunks:
            rows = slice(r0, r0 + n)
            plain = [ring[k, rows, :] for k in range(5)]
            beside = [ring[k, r0 + 1 : r0 + n + 1, :] + ring[k, r0 - 1 : r0 + n - 1, :] for k in range(5)]
            for k in range(4):
                v, zb = plain[k], beside[k]
                vx = (plain[k - 1] if k else swap(v)) + plain[k + 1]
                zx = (beside[k - 1] if k else swap(zb)) + beside[k + 1]
                line_y = v + EDGE * (zb + vx) + CORNER * zx
                total = 2.0 * v + (zb + vx) + EDGE * zx + (y_up(line_y) + y_down(line_y))
                f8 = total * inv[k, rows, :]
                mask = inm[k, rows, :]
                for g in range(NPROJ):
                    t = jnp.tanh(f8 - etas[g])
                    value = t * scales[g] + tops[g]
                    square = value * value
                    hh[g, k, rows, :] = ((0.5 * (1.0 - EMIN)) * (square * value) + 0.5 * EMIN) * mask
                    if k == 0:
                        kk[g, rows, :] = (weights[g] * square) * (1.0 - t * t)

    def precondition(chunks):
        for g in range(NPROJ):
            for k in range(3):
                for r0, n in chunks:
                    rows = slice(r0, r0 + n)
                    h = hh[g, k, rows, :]
                    inner = hh[g, k - 1, rows, :] if k else swap(h)
                    near_h = [
                        inner,
                        hh[g, k + 1, rows, :],
                        y_up(h),
                        y_down(h),
                        hh[g, k, r0 + 1 : r0 + n + 1, :],
                        hh[g, k, r0 - 1 : r0 + n - 1, :],
                    ]
                    diag = sr[k, rows, :]
                    if k == 2:
                        diag = diag + 6.0 * h
                    for i, other in enumerate(near_h):
                        if k < 2:
                            other = h + other
                            cond[g, k, i, rows, :] = other
                        diag = diag + other
                    inverse = inm[k, rows, :] / diag
                    zz[g, k, rows, :] = lr[k, rows, :] * inverse
                    if k < 2:
                        idg[g, k, rows, :] = inverse

    def others(field, g, k, r0, n, v):
        rows = slice(r0, r0 + n)
        return [
            field[g, k - 1, rows, :] if k else swap(v),
            field[g, k + 1, rows, :],
            y_up(v),
            y_down(v),
            field[g, k, r0 + 1 : r0 + n + 1, :],
            field[g, k, r0 - 1 : r0 + n - 1, :],
        ]

    def operate(field, g, k, r0, n):
        v = field[g, k, r0 : r0 + n, :]
        total = None
        for i, other in enumerate(others(field, g, k, r0, n, v)):
            term = cond[g, k, i, r0 : r0 + n, :] * (v - other)
            total = term if total is None else total + term
        return v, total

    sums = [[None] * 4 for _ in range(NPROJ)]

    def add(g, i, r0, n, v):
        v = v[max(LO - r0, 0) : n - max(r0 + n - HI, 0)]
        v = jnp.sum(v.reshape(v.shape[0] // 8, 8, 128), axis=0)
        sums[g][i] = v if sums[g][i] is None else sums[g][i] + v

    def first_step(chunks):
        for g in range(NPROJ):
            for k in range(2):
                for r0, n in chunks:
                    rows = slice(r0, r0 + n)
                    v, image = operate(zz, g, k, r0, n)
                    w = image * idg[g, k, rows, :]
                    ww[g, k, rows, :] = w
                    if k == 0:
                        add(g, 0, r0, n, v * lr[0, rows, :])
                        add(g, 1, r0, n, v * image)
                        add(g, 2, r0, n, w * image)

    def second_step(chunks):
        for g in range(NPROJ):
            for r0, n in chunks:
                w, image = operate(ww, g, 0, r0, n)
                add(g, 3, r0, n, w * image)

    project(FILTER[0])

    all_marks.wait_recv()

    for r0, n in ALL:
        rows = slice(r0, r0 + n)
        for k in range(3):
            mask = inm[k, rows, :]
            both = []
            for i in range(2):
                if k == 0:
                    both.append(lt[i, r0 + 8 + THICK - LO : r0 + n + 8 + THICK - LO, :])
                elif k == 1:
                    both.append(swap(jnp.where(upper, ls[0, i, rows, :], ls[1, i, rows, :])))
                else:
                    both.append(jnp.where(upper, ls[1, i, rows, :], ls[0, i, rows, :]))
            lr[k, rows, :] = both[0] * mask
            sr[k, rows, :] = PENALTY * jnp.maximum(both[1], 1.0 - mask)

    precondition(DIAGONAL[0])
    first_step(FIRST[0])
    second_step(SECOND[0])

    all_rims.wait_recv()
    for j, r0 in enumerate((LO - REACH, HI)):
        form_rings(r0, REACH, [rim_in[i, j] for i in range(5)])
    project(FILTER[1])
    precondition(DIAGONAL[1])
    first_step(FIRST[1])
    second_step(SECOND[1])

    parts = jnp.concatenate([jnp.sum(sums[g][i], axis=0, keepdims=True) for i in range(4) for g in range(NPROJ)] + [jnp.zeros((4, 128), F32)], axis=0)
    totals = jnp.sum(parts, axis=1, keepdims=True)
    which = lax.broadcasted_iota(jnp.int32, (16, 128), 0)
    place = (which // NPROJ) * 32 + which % NPROJ
    spot = lax.broadcasted_iota(jnp.int32, (16, 128), 1)
    line = jnp.sum(jnp.where((spot == place) & (which < 12), totals, 0.0), axis=0, keepdims=True)

    def share(value, rows_ref, ssem, rsem, places):
        rows_ref[0] = value
        for d, place in enumerate(places):
            remote(rows_ref.at[0], rows_ref.at[d + 1], ssem.at[0], rsem.at[0], place).start()
        every = rows_ref.at[pl.ds(1, len(places))]
        return remote(every, every, ssem.at[0], rsem.at[0], places[0])

    def gathered(rows_ref, size):
        terms = [rows_ref[d] for d in range(size)]
        while len(terms) > 1:
            terms = [a + b for a, b in zip(terms[::2], terms[1::2])] + terms[len(terms) // 2 * 2 :]
        return terms[0]

    in_plane = share(line, rowz, send_z, recv_z, stack)
    for item in (all_main, all_rims, all_small, all_marks):
        item.wait_send()

    for g in range(NPROJ):
        for r0, n in OWN:
            rows = slice(r0, r0 + n)
            v, w = zz[g, 0, rows, :], ww[g, 0, rows, :]
            forms = [None] * 3
            for a, b in zip(others(zz, g, 0, r0, n, v), others(ww, g, 0, r0, n, w)):
                gap_v, gap_w = v - a, w - b
                for i, term in enumerate((gap_v * gap_v, gap_v * gap_w, gap_w * gap_w)):
                    forms[i] = term if forms[i] is None else forms[i] + term
            for i in range(3):
                ee[g, i, r0 - LO : r0 - LO + n, :] = forms[i] * kk[g, rows, :]
        for i in range(3):
            turned_e[g, i] = ee[g, i].T

    in_plane.wait_recv()
    in_stack = share(gathered(rowz, NZC * NCORE), rowp, send_p, recv_p, plane)
    in_plane.wait_send()
    in_stack.wait_recv()
    line = gathered(rowp, NXC * NYC)

    rz0, pq1 = line, pltpu.roll(line, 96, 1)
    qdq, wsw = pltpu.roll(line, 64, 1), pltpu.roll(line, 32, 1)
    step_one = rz0 / pq1
    rz1 = rz0 - 2.0 * step_one * pq1 + step_one * step_one * qdq
    grow = 1.0 + rz1 / rz0
    pq2 = grow * grow * pq1 - 2.0 * grow * step_one * qdq + step_one * step_one * wsw
    step_two = rz1 / pq2
    along = step_one + step_two * grow
    across = -step_one * step_two

    scale = (along * along, 2.0 * along * across, across * across)
    factors = [[jnp.broadcast_to(part[:, g : g + 1], (1, 128)) for part in scale] for g in range(NPROJ)]
    for layer in range(DEPTH):
        for y in range(0, WIDTH, 32):
            rows = slice(layer * WIDTH + y, layer * WIDTH + y + 32)
            result = None
            for g in range(NPROJ):
                for i in range(3):
                    term = factors[g][i] * turned_e[g, i, rows, :]
                    result = term if result is None else result + term
            out[layer, y : y + 32, :] = result

    in_stack.wait_send()


def local(design, solid_mask, void_mask, load_mask, support_mask, thresholds, group_weight):
    dma = pltpu.SemaphoreType.DMA
    return pl.pallas_call(
        kernel,
        out_shape=pltpu.VMEM((DEPTH, WIDTH, THICK), F32),
        in_specs=[pl.BlockSpec(memory_space=pl.ANY)] * 5 + [pl.BlockSpec(memory_space=pltpu.HBM)] * 2,
        out_specs=pl.BlockSpec(memory_space=pltpu.VMEM),
        scratch_shapes=[
            pltpu.VMEM((DEPTH, WIDTH, THICK), F32),
            pltpu.VMEM((8, DEPTH, WIDTH, THICK), jnp.int32),
            pltpu.VMEM((5, ROWS, 128), F32),
            pltpu.VMEM((2, REACH, 128), F32),
            pltpu.VMEM((5, 2, REACH, 128), F32),
            pltpu.VMEM((2, 3 * THICK + 16, 128), F32),
            pltpu.VMEM((2, 2, ROWS, 128), F32),
            pltpu.VMEM((5, ROWS, 128), F32),
            pltpu.VMEM((3, ROWS, 128), F32),
            pltpu.VMEM((3, ROWS, 128), F32),
            pltpu.VMEM((5, ROWS, 128), F32),
            pltpu.VMEM((4, ROWS, 128), F32),
            pltpu.VMEM((NPROJ, 8, 128), F32),
            pltpu.VMEM((NPROJ, 4, ROWS, 128), F32),
            pltpu.VMEM((NPROJ, 2, 6, ROWS, 128), F32),
            pltpu.VMEM((NPROJ, 3, ROWS, 128), F32),
            pltpu.VMEM((NPROJ, 2, ROWS, 128), F32),
            pltpu.VMEM((NPROJ, 2, ROWS, 128), F32),
            pltpu.VMEM((NPROJ, ROWS, 128), F32),
            pltpu.VMEM((NXC * NYC, 1, 128), F32),
            pltpu.VMEM((NZC * NCORE, 1, 128), F32),
            pltpu.VMEM((NPROJ, 3, THICK, 128), F32),
            pltpu.VMEM((NPROJ, 3, THICK, 128), F32),
            pltpu.SMEM((1, 1), jnp.int32),
            pltpu.SMEM((1, 1), F32),
            dma((5,)), dma((1,)),
            dma((1,)), dma((4,)),
            dma((1,)), dma((1,)),
            dma((1,)), dma((1,)),
            dma((1,)), dma((1,)),
            dma((1,)), dma((1,)),
            dma((1,)), dma((1,)),
        ],
        compiler_params=pltpu.CompilerParams(collective_id=0, has_side_effects=True),
    )(
        design, solid_mask, void_mask, load_mask, support_mask,
        thresholds.reshape(1, 1), group_weight.reshape(1, 1),
    )


def solution(mesh):
    placed = (
        P("space", None, "proj"),
        P("space", None, "proj"),
        P("space", None, "proj"),
        P("space", None, None),
        P("space", None, None),
        P("proj"),
        P("proj"),
    )
    return jax.shard_map(
        local, mesh=mesh, in_specs=placed, out_specs=P("space", None, "proj"), check_vma=False
    )
```
